512 devices in a mesh: section: 4 (over x), tile: 128 (over z, y, core).
Axes of the slice: x: 4, y: 8, z: 8, core: 2. Of those that a mesh axis runs over, the one named last changes fastest.
Arguments:
- features: bfloat16 [512, 16, 16, 256], P('tile'), may hold values from -6 to 6
- out_cotangent: bfloat16 [512, 16, 16, 256], P('tile'), may hold values from -24 to 24
- w_reduce: bfloat16 [4, 256, 64], P('section'), may hold values from -0.375 to 0.375
- w_taps: bfloat16 [4, 576, 64], P('section'), may hold values from -0.25 to 0.25
- w_expand: bfloat16 [4, 64, 256], P('section'), may hold values from -0.75 to 0.75
- norm_scale: float32 [4, 384], P('section'), may hold values from 0.25 to 1.75
- norm_shift: float32 [4, 384], P('section'), may hold values from -2 to 2
- owner: int32 [512], replicated, may hold values from 0 to 511, as said below
- neighbours: int32 [512, 4], replicated, may hold values from -1 to 511, as said below
Outputs:
- block_outputs: bfloat16 [4, 512, 16, 16, 256], P('section', 'tile')
- input_grads: bfloat16 [4, 512, 16, 16, 256], P('section', 'tile')
- grad_reduce: float32 [4, 256, 64], P('section')
- grad_taps: float32 [4, 576, 64], P('section')
- grad_expand: float32 [4, 64, 256], P('section')
The draws below stay inside these ranges and needn't reach their ends.
Inputs may be any that keep to these rules, and one draw needn't show every extreme that they name: `owner`: A permutation of the rows; the rows 4 k to 4 k + 3 belong to index k of tile. The tiles form a band 8 tiles across; two neighbouring tiles are owned by indices of tile at most 3 apart, and west and east neighbours by indices at most 1 apart. Symmetric: if neighbours[t, 0] = u then neighbours[u, 1] = t, and likewise for west and east; -1 at the band's border.
All inputs are finite; a program needn't handle non-finite values.
Results may differ from the reference program's by a relative error of at most 0.039.
Values may be sent and summed in bfloat16 or wider, within the bound.
No kernel may reach another device: no remote copies, remote signals or barrier semaphores. Data moves between devices by JAX's collectives and lax.ppermute only.
A program may use at most 64 MiB of HBM per device.

```python
import jax
import jax.numpy as jnp
import numpy as np
from jax import lax

C = 256
M = 64
P_SIZE = 16
TILE_DEV = 4
BLOCKS = 4
BAND_W = 8
TILES = 512
NORM = 384


def band_layout(key):
    key_ids = jax.random.fold_in(key, 101)
    key_mix = jax.random.fold_in(key, 202)
    ids = jax.random.permutation(key_ids, TILES).astype(jnp.int32)
    group = 2 * TILE_DEV
    groups = TILES // group
    scores = jax.random.randint(key_mix, (groups, group), 0, 1 << 20).astype(jnp.int32) * group
    scores = scores + jnp.arange(group, dtype=jnp.int32)[None, :]
    within = jnp.argsort(scores, axis=1).astype(jnp.int32)
    slot_of_pos = (jnp.arange(groups, dtype=jnp.int32)[:, None] * group + within).reshape(-1)
    position = jnp.arange(TILES, dtype=jnp.int32)
    row = position // BAND_W
    col = position % BAND_W
    rows = TILES // BAND_W
    north = jnp.where(row > 0, position - BAND_W, -1)
    south = jnp.where(row < rows - 1, position + BAND_W, -1)
    west = jnp.where(col > 0, position - 1, -1)
    east = jnp.where(col < BAND_W - 1, position + 1, -1)
    near_pos = jnp.stack([north, south, west, east], axis=1)
    near_ids = jnp.where(near_pos >= 0, jnp.take(ids, jnp.maximum(near_pos, 0)), -1).astype(jnp.int32)
    owner = jnp.zeros((TILES,), jnp.int32).at[ids].set(slot_of_pos)
    neighbours = jnp.zeros((TILES, 4), jnp.int32).at[ids].set(near_ids)
    return (owner, neighbours)


def draw_owner(key, part):
    return band_layout(key)[0]


def draw_neighbours(key, part):
    return band_layout(key)[1]


def raised(entries, own_key, source, target, blocks, factor):
    def block_of(axis_at):
        return (jnp.arange(entries.shape[axis_at]) // (entries.shape[axis_at] // blocks)).reshape((-1,) + (1,) * (entries.ndim - 1 - axis_at))

    first = jax.random.permutation(own_key, blocks)[block_of(target)]
    second = (block_of(target) + blocks // 2) % blocks
    return jnp.where((block_of(source) == first) | (block_of(source) == second), factor * entries, entries)


def steps_of(rng, dims, cuts, smallest, top_value):
    level, own = 1.0, jax.random.fold_in(rng, 6)
    for dim, blocks in cuts:
        draws = jnp.exp(jax.random.uniform(jax.random.fold_in(own, dim), (blocks,), jnp.float32, smallest / len(cuts), top_value / len(cuts)))
        level = level * jnp.repeat(draws, dims[dim] // blocks).reshape([-1 if axis == dim else 1 for axis in range(len(dims))])
    return level


def bell_draw(own_key, shape, deviation, most, cuts=(), kind=jnp.bfloat16):
    values = jax.random.normal(own_key, shape, jnp.float32) * deviation
    if len(cuts) > 0:
        values = steps_of(own_key, shape, cuts, -0.22, 0.18) * values
    return jnp.clip(values, min=-most, max=most).astype(kind)


def noise_with(own_key, shape, spread, reach, cuts, heavy, held_as=jnp.bfloat16):
    values = spread * jax.random.normal(own_key, shape, jnp.float32)
    if cuts:
        values = values * steps_of(own_key, shape, cuts, -0.22, 0.18)
    return jnp.clip(raised(values, jax.random.fold_in(own_key, 3), *heavy), -reach, reach).astype(held_as)


def setup_inputs(seed: int = 0) -> dict:
    splits = jax.random.split(jax.random.key(seed), 10)
    features = bell_draw(splits[0], (TILES, P_SIZE, P_SIZE, C), 1.0, 6.0, ((0, 128),))
    out_cotangent = noise_with(splits[1], (TILES, P_SIZE, P_SIZE, C), 1.0, 24.0, ((0, 128),), (0, 3, 128, 5.5))
    w_reduce = bell_draw(splits[2], (BLOCKS, C, M), C ** -0.5, 0.375, ((0, 4),))
    w_taps = bell_draw(splits[3], (BLOCKS, 9 * M, M), (9 * M) ** -0.5, 0.25, ((0, 4),))
    w_expand = bell_draw(splits[4], (BLOCKS, M, C), M ** -0.5, 0.75, ((0, 4),))
    norm_scale = jnp.clip(1.0 + 0.15 * jax.random.normal(splits[5], (BLOCKS, NORM), jnp.float32), 0.25, 1.75)
    norm_shift = bell_draw(splits[6], (BLOCKS, NORM), 0.3, 2.0, ((0, 4),), jnp.float32)
    owner = draw_owner(jax.random.fold_in(splits[9], 71), 0)
    neighbours = draw_neighbours(jax.random.fold_in(splits[9], 71), 0)
    return dict(features=features, out_cotangent=out_cotangent, w_reduce=w_reduce, w_taps=w_taps, w_expand=w_expand, norm_scale=norm_scale, norm_shift=norm_shift, owner=owner, neighbours=neighbours)


OPPOSITE = np.array([1, 0, 3, 2], dtype=np.int32)

def silu_grad(value):
    sig = jax.nn.sigmoid(value)
    return sig * (1.0 + value * (1.0 - sig))

def inner_product(left, right):
    return lax.dot_general(left, right, (((0,), (0,)), ((), ())), preferred_element_type=jnp.float32)

def times_transposed(left, right):
    return lax.dot_general(left, right, (((1,), (1,)), ((), ())), preferred_element_type=jnp.float32)

def face_targets(owner, neighbours, slots):
    tiles = owner.shape[0]
    hit = owner[None, :] == slots[:, None]
    tile_ids = lax.optimization_barrier(jnp.sum(jnp.where(hit, jnp.arange(tiles, dtype=jnp.int32)[None, :], 0), axis=1)).astype(jnp.int32)
    near = jnp.take(neighbours, tile_ids, axis=0)
    valid = near >= 0
    near_slot = jnp.take(owner, jnp.where(valid, near, 0), axis=0).astype(jnp.int32)
    return (near_slot, valid)

def edge_rows(field):
    count, side, _, width = field.shape
    rows = jnp.stack([field[:, 0], field[:, side - 1], field[:, :, 0], field[:, :, side - 1]], axis=1)
    return rows.reshape(count, 4, side * width)

def halo_rows(d_padded):
    count = d_padded.shape[0]
    width = d_padded.shape[3]
    side = d_padded.shape[1] - 2
    rows = jnp.stack([d_padded[:, 0, 1:-1], d_padded[:, -1, 1:-1], d_padded[:, 1:-1, 0], d_padded[:, 1:-1, -1]], axis=1)
    return rows.reshape(count, 4, side * width)

def with_faces(hidden, faces):
    count, side, _, width = hidden.shape
    faces = faces.reshape(count, 4, side, width)
    middle = jnp.concatenate([faces[:, 2][:, :, None], hidden, faces[:, 3][:, :, None]], axis=2)
    corner = jnp.zeros((count, 1, 1, width), hidden.dtype)
    top = jnp.concatenate([corner, faces[:, 0][:, None], corner], axis=2)
    bottom = jnp.concatenate([corner, faces[:, 1][:, None], corner], axis=2)
    return jnp.concatenate([top, middle, bottom], axis=1)

def reduce_front(inputs, w_red, scale, shift):
    count, side, _, chans = inputs.shape
    width = w_red.shape[1]
    pre1 = jnp.dot(inputs.reshape(-1, chans), w_red, preferred_element_type=jnp.float32) * scale[:width] + shift[:width]
    return (pre1, jax.nn.silu(pre1).astype(jnp.bfloat16).reshape(count, side, side, width))

def block_tail(inputs, padded, w_tap, w_exp, scale, shift):
    side = inputs.shape[1]
    chans = inputs.shape[3]
    width = w_tap.shape[1]
    parts = [padded[:, dy:dy + side, dx:dx + side, :] for dy in range(3) for dx in range(3)]
    columns = jnp.concatenate(parts, axis=-1).reshape(-1, 9 * width)
    pre2 = jnp.dot(columns, w_tap, preferred_element_type=jnp.float32) * scale[width:2 * width] + shift[width:2 * width]
    hidden2 = jax.nn.silu(pre2).astype(jnp.bfloat16)
    expanded = jnp.dot(hidden2, w_exp, preferred_element_type=jnp.float32)
    pre3 = inputs.reshape(-1, chans).astype(jnp.float32) + expanded * scale[2 * width:] + shift[2 * width:]
    return (columns, pre2, hidden2, pre3)

def block_forward(inputs, params, fetch):
    w_red, w_tap, w_exp, scale, shift = params
    pre1, hidden1 = reduce_front(inputs, w_red, scale, shift)
    padded = with_faces(hidden1, fetch(edge_rows(hidden1)))
    columns, pre2, hidden2, pre3 = block_tail(inputs, padded, w_tap, w_exp, scale, shift)
    return (jax.nn.silu(pre3).astype(jnp.bfloat16).reshape(inputs.shape), padded)

def block_backward(inputs, padded, upstream, params, fetch):
    w_red, w_tap, w_exp, scale, shift = params
    count, side, _, chans = inputs.shape
    width = w_tap.shape[1]
    pre1, hidden1 = reduce_front(inputs, w_red, scale, shift)
    columns, pre2, hidden2, pre3 = block_tail(inputs, padded, w_tap, w_exp, scale, shift)
    d_pre3 = upstream.reshape(pre3.shape).astype(jnp.float32) * silu_grad(pre3)
    e_three = (d_pre3 * scale[2 * width:]).astype(jnp.bfloat16)
    g_expand = inner_product(hidden2, e_three)
    d_two = (times_transposed(e_three, w_exp) * silu_grad(pre2) * scale[width:2 * width]).astype(jnp.bfloat16)
    g_taps = inner_product(columns, d_two)
    d_columns = times_transposed(d_two, w_tap).reshape(count, side, side, 9 * width)
    d_padded = jnp.zeros((count, side + 2, side + 2, width), jnp.float32)
    for tap in range(9):
        dy, dx = (tap // 3, tap % 3)
        piece = d_columns[..., tap * width:(tap + 1) * width]
        d_padded = d_padded + jnp.pad(piece, ((0, 0), (dy, 2 - dy), (dx, 2 - dx), (0, 0)))
    d_padded = d_padded.astype(jnp.bfloat16)
    received = fetch(halo_rows(d_padded)).reshape(count, 4, side, width).astype(jnp.float32)
    d_hidden = d_padded[:, 1:-1, 1:-1].astype(jnp.float32)
    d_hidden = d_hidden.at[:, 0].add(received[:, 0])
    d_hidden = d_hidden.at[:, side - 1].add(received[:, 1])
    d_hidden = d_hidden.at[:, :, 0].add(received[:, 2])
    d_hidden = d_hidden.at[:, :, side - 1].add(received[:, 3])
    d_one = (d_hidden.reshape(-1, width) * silu_grad(pre1) * scale[:width]).astype(jnp.bfloat16)
    g_reduce = inner_product(inputs.reshape(-1, chans), d_one)
    d_inputs = (d_pre3 + times_transposed(d_one, w_red)).astype(jnp.bfloat16).reshape(inputs.shape)
    return (d_inputs, (g_reduce, g_taps, g_expand))

def reference(features, out_cotangent, w_reduce, w_taps, w_expand, norm_scale, norm_shift, owner, neighbours):
    tiles = features.shape[0]
    blocks = w_reduce.shape[0]
    slots = jnp.arange(tiles, dtype=jnp.int32)
    near_slot, valid = face_targets(owner, neighbours, slots)
    place = jnp.where(valid, near_slot * 4 + OPPOSITE[None, :], 0).astype(jnp.int32)

    def fetch(edges):
        pool = edges.reshape(-1, edges.shape[-1])
        picked = jnp.take(pool, place.reshape(-1), axis=0).reshape(edges.shape)
        return jnp.where(valid[..., None], picked, jnp.zeros_like(picked))
    held = features
    inputs_list, pads, outs = ([], [], [])
    for step in range(blocks):
        params = (w_reduce[step], w_taps[step], w_expand[step], norm_scale[step], norm_shift[step])
        result, padded = block_forward(held, params, fetch)
        inputs_list.append(held)
        pads.append(padded)
        outs.append(result)
        held = result
    upstream = out_cotangent
    d_list = [None] * blocks
    g_lists = [None] * blocks
    for step in reversed(range(blocks)):
        params = (w_reduce[step], w_taps[step], w_expand[step], norm_scale[step], norm_shift[step])
        d_inputs, grads = block_backward(inputs_list[step], pads[step], upstream, params, fetch)
        d_list[step] = d_inputs
        g_lists[step] = grads
        upstream = d_inputs
    return (jnp.stack(outs), jnp.stack(d_list), jnp.stack([g[0] for g in g_lists]), jnp.stack([g[1] for g in g_lists]), jnp.stack([g[2] for g in g_lists]))
```

```python
from functools import partial

import jax
import jax.numpy as jnp
import numpy as np
from jax import lax
from jax.sharding import Mesh
from jax.sharding import PartitionSpec as P

REACH = 3
TILE_AXES = ("z", "y", "core")


OPPOSITE = np.array([1, 0, 3, 2], dtype=np.int32)


def from_behind(block, axis, distance):
    devices = range(lax.axis_size(axis))
    route = [(i - distance, i) for i in devices if i - distance in devices]
    return lax.ppermute(block, axis, route)


def silu_grad(value):
    sig = jax.nn.sigmoid(value)
    return sig * (1.0 + value * (1.0 - sig))


def inner_product(left, right):
    return lax.dot_general(
        left, right, (((0,), (0,)), ((), ())), preferred_element_type=jnp.float32
    )


def times_transposed(left, right):
    return lax.dot_general(
        left, right, (((1,), (1,)), ((), ())), preferred_element_type=jnp.float32
    )


def face_targets(owner, neighbours, slots):
    tiles = owner.shape[0]
    hit = owner[None, :] == slots[:, None]
    tile_ids = jnp.sum(jnp.where(hit, jnp.arange(tiles, dtype=jnp.int32)[None, :], 0), axis=1)
    near = jnp.take(neighbours, tile_ids, axis=0)
    valid = near >= 0
    near_slot = jnp.take(owner, jnp.where(valid, near, 0), axis=0)
    return (near_slot, valid)


def edge_rows(field):
    count, side, _, width = field.shape
    rows = jnp.stack(
        [field[:, 0], field[:, side - 1], field[:, :, 0], field[:, :, side - 1]], axis=1
    )
    return rows.reshape(count, 4, side * width)


def halo_rows(d_padded):
    count = d_padded.shape[0]
    width = d_padded.shape[3]
    side = d_padded.shape[1] - 2
    rows = jnp.stack(
        [d_padded[:, 0, 1:-1], d_padded[:, -1, 1:-1], d_padded[:, 1:-1, 0], d_padded[:, 1:-1, -1]],
        axis=1,
    )
    return rows.reshape(count, 4, side * width)


def with_faces(hidden, faces):
    count, side, _, width = hidden.shape
    faces = faces.reshape(count, 4, side, width)
    middle = jnp.concatenate([faces[:, 2][:, :, None], hidden, faces[:, 3][:, :, None]], axis=2)
    corner = jnp.zeros((count, 1, 1, width), hidden.dtype)
    top = jnp.concatenate([corner, faces[:, 0][:, None], corner], axis=2)
    bottom = jnp.concatenate([corner, faces[:, 1][:, None], corner], axis=2)
    return jnp.concatenate([top, middle, bottom], axis=1)


def reduce_front(inputs, w_red, scale, shift):
    count, side, _, chans = inputs.shape
    width = w_red.shape[1]
    pre1 = (
        jnp.dot(inputs.reshape(-1, chans), w_red, preferred_element_type=jnp.float32)
        * scale[:width]
        + shift[:width]
    )
    return (pre1, jax.nn.silu(pre1).astype(jnp.bfloat16).reshape(count, side, side, width))


def block_tail(inputs, padded, w_tap, w_exp, scale, shift):
    side = inputs.shape[1]
    chans = inputs.shape[3]
    width = w_tap.shape[1]
    parts = [padded[:, dy : dy + side, dx : dx + side, :] for dy in range(3) for dx in range(3)]
    columns = jnp.concatenate(parts, axis=-1).reshape(-1, 9 * width)
    pre2 = (
        jnp.dot(columns, w_tap, preferred_element_type=jnp.float32) * scale[width : 2 * width]
        + shift[width : 2 * width]
    )
    hidden2 = jax.nn.silu(pre2).astype(jnp.bfloat16)
    expanded = jnp.dot(hidden2, w_exp, preferred_element_type=jnp.float32)
    pre3 = (
        inputs.reshape(-1, chans).astype(jnp.float32)
        + expanded * scale[2 * width :]
        + shift[2 * width :]
    )
    return (columns, pre2, hidden2, pre3)


def block_forward(inputs, params, fetch):
    w_red, w_tap, w_exp, scale, shift = params
    pre1, hidden1 = reduce_front(inputs, w_red, scale, shift)
    padded = with_faces(hidden1, fetch(edge_rows(hidden1)))
    columns, pre2, hidden2, pre3 = block_tail(inputs, padded, w_tap, w_exp, scale, shift)
    return (jax.nn.silu(pre3).astype(jnp.bfloat16).reshape(inputs.shape), padded)


def block_backward(inputs, padded, upstream, params, fetch):
    w_red, w_tap, w_exp, scale, shift = params
    count, side, _, chans = inputs.shape
    width = w_tap.shape[1]
    pre1, hidden1 = reduce_front(inputs, w_red, scale, shift)
    columns, pre2, hidden2, pre3 = block_tail(inputs, padded, w_tap, w_exp, scale, shift)
    d_pre3 = upstream.reshape(pre3.shape).astype(jnp.float32) * silu_grad(pre3)
    e_three = (d_pre3 * scale[2 * width :]).astype(jnp.bfloat16)
    g_expand = inner_product(hidden2, e_three)
    d_two = (times_transposed(e_three, w_exp) * silu_grad(pre2) * scale[width : 2 * width]).astype(
        jnp.bfloat16
    )
    g_taps = inner_product(columns, d_two)
    d_columns = times_transposed(d_two, w_tap).reshape(count, side, side, 9 * width)
    d_padded = jnp.zeros((count, side + 2, side + 2, width), jnp.float32)
    for tap in range(9):
        dy, dx = (tap // 3, tap % 3)
        piece = d_columns[..., tap * width : (tap + 1) * width]
        d_padded = d_padded + jnp.pad(piece, ((0, 0), (dy, 2 - dy), (dx, 2 - dx), (0, 0)))
    d_padded = d_padded.astype(jnp.bfloat16)
    received = fetch(halo_rows(d_padded)).reshape(count, 4, side, width).astype(jnp.float32)
    d_hidden = d_padded[:, 1:-1, 1:-1].astype(jnp.float32)
    d_hidden = d_hidden.at[:, 0].add(received[:, 0])
    d_hidden = d_hidden.at[:, side - 1].add(received[:, 1])
    d_hidden = d_hidden.at[:, :, 0].add(received[:, 2])
    d_hidden = d_hidden.at[:, :, side - 1].add(received[:, 3])
    d_one = (d_hidden.reshape(-1, width) * silu_grad(pre1) * scale[:width]).astype(jnp.bfloat16)
    g_reduce = inner_product(inputs.reshape(-1, chans), d_one)
    d_inputs = (d_pre3 + times_transposed(d_one, w_red)).astype(jnp.bfloat16).reshape(inputs.shape)
    return (d_inputs, (g_reduce, g_taps, g_expand))


def collect(edges, near_slot, valid):
    count, _, length = edges.shape
    here = lax.axis_index(TILE_AXES)
    edges = edges.reshape(count * 4, length // 128, 128)
    gap = near_slot // count - here
    place = ((gap + REACH) * count + near_slot % count) * 4 + OPPOSITE[None, :]
    pieces = []
    for offset in range(-REACH, REACH + 1):
        pieces.append(edges if offset == 0 else from_behind(edges, TILE_AXES, -offset))
    pool = jnp.concatenate(pieces)
    place = jnp.where(valid, place, 0).astype(jnp.int32)
    picked = jnp.take(pool, place.reshape(-1), axis=0).reshape(near_slot.shape + (length,))
    return jnp.where(valid[..., None], picked, jnp.zeros_like(picked))


def swap_chunks(parts, axes):
    return lax.all_to_all(parts, axes, 0, 0, tiled=True)


def sum_over_tiles(values):
    plane = ("y", "core")
    across = lax.axis_size(plane)
    deep = lax.axis_size("z")
    parts = values.astype(jnp.bfloat16).reshape(across, -1)
    mine = jnp.sum(swap_chunks(parts, plane).astype(jnp.float32), axis=0)
    copies = jnp.broadcast_to(mine.astype(jnp.bfloat16)[None], (deep,) + mine.shape)
    total = jnp.sum(swap_chunks(copies, "z").astype(jnp.float32), axis=0)
    copies = jnp.broadcast_to(total.astype(jnp.bfloat16)[None], (across,) + total.shape)
    return swap_chunks(copies, plane).astype(jnp.float32).reshape(-1)


def split_float(value):
    high = value.astype(jnp.bfloat16)
    low = (value - high.astype(jnp.float32)).astype(jnp.bfloat16)
    return (high, low)


def gather_params(w_reduce, w_taps, w_expand, norm_scale, norm_shift):
    pieces = [w_reduce, w_taps, w_expand]
    for item in (norm_scale, norm_shift):
        pieces.extend(split_float(item))
    packed = jnp.concatenate([item.reshape(-1, 128) for item in pieces])
    every = lax.all_gather(packed, "section", axis=0, tiled=False)
    at = 0
    cut = []
    for item in pieces:
        rows = item.size // 128
        cut.append(every[:, at : at + rows].reshape((-1,) + item.shape[1:]))
        at += rows
    scale = cut[3].astype(jnp.float32) + cut[4].astype(jnp.float32)
    shift = cut[5].astype(jnp.float32) + cut[6].astype(jnp.float32)
    return (cut[0], cut[1], cut[2], scale, shift)


def on_device(
    features, out_cotangent, w_reduce, w_taps, w_expand, norm_scale, norm_shift, owner, neighbours
):
    blocks = lax.axis_size("section")
    count = features.shape[0]
    here = lax.axis_index(TILE_AXES)
    section_here = lax.axis_index("section")
    slots = here * count + jnp.arange(count, dtype=jnp.int32)
    near_slot, valid = face_targets(owner, neighbours, slots)
    fetch = partial(collect, near_slot=near_slot, valid=valid)
    every = gather_params(w_reduce, w_taps, w_expand, norm_scale, norm_shift)
    held = features
    inputs_list, pads, outs = ([], [], [])
    for step in range(blocks):
        params = tuple((item[step] for item in every))
        result, padded = block_forward(held, params, fetch)
        inputs_list.append(held)
        pads.append(padded)
        outs.append(result)
        held = result
    upstream = out_cotangent
    d_list = [None] * blocks
    g_lists = [None] * blocks
    for step in reversed(range(blocks)):
        params = tuple((item[step] for item in every))
        d_inputs, new_grads = block_backward(inputs_list[step], pads[step], upstream, params, fetch)
        d_list[step] = d_inputs
        g_lists[step] = new_grads
        upstream = d_inputs
    outputs = lax.select_n(section_here, *outs)[None]
    input_grads = lax.select_n(section_here, *d_list)[None]
    grads = [lax.select_n(section_here, *[g[i] for g in g_lists]) for i in range(3)]
    total = sum_over_tiles(jnp.concatenate([g.reshape(-1) for g in grads]))
    ends = np.cumsum([g.size for g in grads])
    cuts = [total[e - g.size : e].reshape((1,) + g.shape) for e, g in zip(ends, grads)]
    return (outputs, input_grads, cuts[0], cuts[1], cuts[2])


def fine_mesh(mesh):
    return Mesh(
        mesh.devices.reshape(mesh.devices.shape[0], 8, 8, 2), ("section",) + TILE_AXES
    )


def solution(mesh):
    return jax.shard_map(
        on_device,
        mesh=fine_mesh(mesh),
        in_specs=(
            P(TILE_AXES, None, None, None),
            P(TILE_AXES, None, None, None),
            P("section", None, None),
            P("section", None, None),
            P("section", None, None),
            P("section", None),
            P("section", None),
            P(),
            P(),
        ),
        out_specs=(
            P("section", TILE_AXES, None, None, None),
            P("section", TILE_AXES, None, None, None),
            P("section", None, None),
            P("section", None, None),
            P("section", None, None),
        ),
        check_vma=False,
    )
```

```python
import jax
import jax.numpy as jnp
import numpy as np
from jax import lax
from jax.experimental import pallas as pl
from jax.experimental.pallas import tpu as pltpu
from jax.sharding import Mesh
from jax.sharding import PartitionSpec as P

TILE_AXES = ("z", "y", "core")
SIDE = 16
REGION = 32
HALO = 8
PIXELS = REGION * REGION
WIDTH = 64
CHANS = 256
TAPS = 9
BF = jnp.bfloat16
F32 = jnp.float32
VMEM_LIMIT = 56 * 1024 * 1024


def mm(left, right):
    return jnp.dot(left, right, preferred_element_type=F32)


def mm_first(left, right):
    return lax.dot_general(left, right, (((0,), (0,)), ((), ())), preferred_element_type=F32)


def silu_parts(value):
    sig = 0.5 + 0.5 * jnp.tanh(0.5 * value)
    out = value * sig
    return (out, sig + out * (1.0 - sig))


def around(tile, owner, near, here):
    north, south = (near[tile * 4], near[tile * 4 + 1])
    west, east = (near[tile * 4 + 2], near[tile * 4 + 3])

    def step(first, way, second, other):
        one = jnp.where(first >= 0, near[jnp.maximum(first, 0) * 4 + way], -1)
        two = jnp.where(second >= 0, near[jnp.maximum(second, 0) * 4 + other], -1)
        return jnp.where(one >= 0, one, two)

    ids = [
        step(north, 2, west, 0), north, step(north, 3, east, 0),
        west, tile, east,
        step(south, 2, west, 1), south, step(south, 3, east, 1),
    ]
    places, found = ([], [])
    for item in ids:
        row = owner[jnp.maximum(item, 0)]
        device = row >> 2
        gap = (device >> 1) - (here >> 1)
        order = 2 * jnp.abs(gap) - jnp.where(gap < 0, 1, 0)
        place = order * 4 + (row & 3) + jnp.where((device & 1) == (here & 1), 0, 20)
        places.append(jnp.clip(place, 0, 39))
        found.append(item >= 0)
    return (places, found)


BANDS = ((0, HALO, 0, HALO), (HALO, SIDE, 3, 0), (HALO + SIDE, HALO, 6, 0))


def build_region(pool, region, lane, places, found):
    for top, rows, first, start in BANDS:
        parts = []
        for k in range(3):
            part = pool[places[first + k], pl.ds(start, rows)].astype(F32)
            part = jnp.where(found[first + k], part, 0.0)
            cut = (slice(HALO, SIDE), slice(0, SIDE), slice(0, HALO))[k]
            parts.append(part[:, cut, :])
        band = jnp.concatenate(parts, axis=1).reshape(rows * REGION, CHANS).astype(BF)
        region[pl.ds(top * REGION, rows * REGION), pl.ds(lane * CHANS, CHANS)] = band


def build_present(present, found_pair):
    for top, rows, first, _ in BANDS:
        shape = (rows * REGION, 2 * WIDTH)
        col = lax.broadcasted_iota(jnp.int32, shape, 0) % REGION
        lane = lax.broadcasted_iota(jnp.int32, shape, 1)
        sides = []
        for found in found_pair:
            flags = [jnp.where(found[first + k], 1.0, 0.0) for k in range(3)]
            sides.append(
                jnp.where(col < HALO, flags[0], jnp.where(col < HALO + SIDE, flags[1], flags[2]))
            )
        present[pl.ds(top * REGION, rows * REGION), :] = jnp.where(lane < WIDTH, sides[0], sides[1])


def build_masks(masks):
    shape = (PIXELS, 2 * WIDTH)
    pixel = lax.broadcasted_iota(jnp.int32, shape, 0)
    row, col = (pixel // REGION, pixel % REGION)
    low, high = (HALO, HALO + SIDE)
    west = (col == low) | (col == high)
    east = (col == low - 1) | (col == high - 1)
    above = (row == low - 1) | (row == high - 1)
    below = (row == low) | (row == high)
    for k, (across, along) in enumerate(
        ((above, west), (above, east), (below, west), (below, east))
    ):
        masks[k] = jnp.where(across & along, 0.0, 1.0).astype(BF)


def store_shifted(shifted, masks, start, value):
    count = value.shape[0]
    rows = pl.ds(start, count)
    left = pltpu.roll(value, 1, 0).astype(BF)
    right = pltpu.roll(value, count - 1, 0).astype(BF)
    shifted[0, rows, :] = left
    shifted[1, rows, :] = value.astype(BF)
    shifted[2, rows, :] = right
    shifted[3, rows, :] = left * masks[0, rows, :]
    shifted[4, rows, :] = right * masks[1, rows, :]
    shifted[5, rows, :] = left * masks[2, rows, :]
    shifted[6, rows, :] = right * masks[3, rows, :]


TAP_SOURCES = ((3, -1), (1, -1), (4, -1), (0, 0), (1, 0), (2, 0), (5, 1), (1, 1), (6, 1))


def columns_at(shifted, start, count):
    return jnp.concatenate(
        [shifted[k, pl.ds(start + dy * REGION, count), :] for k, dy in TAP_SOURCES], axis=1
    )


def load_pool(sources, pool, sems):
    copies, at = ([], 0)
    for k, source in enumerate(sources):
        rows = source.shape[0]
        copies.append(pltpu.make_async_copy(source, pool.at[pl.ds(at, rows)], sems.at[k]))
        at += rows
    for copy in copies:
        copy.start()
    for copy in copies:
        copy.wait()


def inner_tile(region, lane):
    value = region[pl.ds(HALO * REGION, SIDE * REGION), pl.ds(lane * CHANS, CHANS)].astype(F32)
    value = value.reshape(SIDE, REGION, CHANS)[:, HALO : HALO + SIDE, :]
    return value.astype(BF)


INNER = (HALO * REGION, SIDE * REGION)


def forward_kernel(
    meta, owner, near, *refs
):
    sources, refs = (refs[:SOURCES], refs[SOURCES:])
    (w_red, w_tap, w_exp, norms, s_one, s_two, s_three, a_own, h_one, h_two, out,
     pool, sems, region, present, masks, shifted) = refs
    pair = pl.program_id(0)
    here, section = (meta[0], meta[1])

    @pl.when(pair == 0)
    def _():
        load_pool(sources, pool, sems)
        build_masks(masks)

    founds = []
    for lane in range(2):
        places, found = around(meta[2 + pair * 2 + lane], owner, near, here)
        build_region(pool, region, lane, places, found)
        founds.append(found)
    build_present(present, founds)

    def block(b, carry):
        mine = b == section

        @pl.when(mine)
        def _():
            a_own[0] = region[pl.ds(*INNER), :]

        def front(j, c):
            start = pl.multiple_of(j * 256, 256)
            rows = pl.ds(start, 256)
            pre = mm(region[rows, :], w_red[b]) * norms[b, 0:1, :128] + norms[b, 1:2, :128]
            hidden, slope = silu_parts(pre)
            there = present[rows, :]
            s_one[0, b, rows, :] = (slope * there * norms[b, 0:1, :128]).astype(BF)
            store_shifted(shifted, masks, start, hidden * there)
            return c

        lax.fori_loop(0, 4, front, 0)

        def tail(j, c):
            start = pl.multiple_of(REGION + j * 320, 32)
            rows = pl.ds(start, 320)
            pre = mm(columns_at(shifted, start, 320), w_tap[b])
            pre = pre * norms[b, 2:3, :128] + norms[b, 3:4, :128]
            hidden, slope = silu_parts(pre)
            s_two[0, b, rows, :] = (slope * norms[b, 2:3, :128]).astype(BF)
            hidden = hidden.astype(BF)

            @pl.when(mine)
            def _():
                h_two[0, rows, :] = hidden

            pre = (
                region[rows, :].astype(F32)
                + mm(hidden, w_exp[b]) * norms[b, 4:5, :]
                + norms[b, 5:6, :]
            )
            value, slope = silu_parts(pre)
            region[rows, :] = value.astype(BF)
            s_three[0, b, rows, :] = slope.astype(BF)
            return c

        lax.fori_loop(0, 3, tail, 0)

        @pl.when(mine)
        def _():
            h_one[0] = shifted[1]
            out[0] = inner_tile(region, 0)
            out[1] = inner_tile(region, 1)

        return carry

    lax.fori_loop(0, 4, block, 0)


def fold_pair(value, rows, cols):
    return value[:rows, :cols] + value[rows:, cols:]


def backward_kernel(meta, owner, near, *refs):
    sources, refs = (refs[:SOURCES], refs[SOURCES:])
    (w_red, w_tap, w_exp, norms, s_one, s_two, s_three, a_own, h_one, h_two, grad_in, grads,
     pool, sems, region, masks, shifted, d_one, total) = refs
    pair = pl.program_id(0)
    here, section = (meta[0], meta[1])

    @pl.when(pair == 0)
    def _():
        load_pool(sources, pool, sems)
        build_masks(masks)
        total[...] = jnp.zeros_like(total)

    for lane in range(2):
        places, found = around(meta[2 + pair * 2 + lane], owner, near, here)
        build_region(pool, region, lane, places, found)

    def keep_inner(value):
        col = lax.broadcasted_iota(jnp.int32, value.shape, 0) % REGION
        return jnp.where((col >= HALO) & (col < HALO + SIDE), value, 0.0).astype(BF)

    def block(step, carry):
        b = 3 - step
        mine = b == section

        def first(j, c):
            start = pl.multiple_of(4 * REGION + j * 256, 128)
            rows = pl.ds(start, 256)
            d_three = region[rows, :].astype(F32) * s_three[0, b, rows, :].astype(F32)
            e_three = (d_three * norms[b, 4:5, :]).astype(BF)
            d_two = mm(e_three, w_exp[b]) * s_two[0, b, rows, :].astype(F32)
            store_shifted(shifted, masks, start, d_two)
            return c

        lax.fori_loop(0, 3, first, 0)

        @pl.when(mine)
        def _():
            rows = pl.ds(*INNER)
            d_three = region[rows, :].astype(F32) * s_three[0, b, rows, :].astype(F32)
            e_three = keep_inner(d_three * norms[b, 4:5, :])
            total_e = fold_pair(mm_first(h_two[0, rows, :], e_three), WIDTH, CHANS)
            total[416:480, :] += total_e[:, :128]
            total[480:544, :] += total_e[:, 128:]
            d_two = keep_inner(shifted[1, rows, :].astype(F32))
            around_rows = pl.ds(INNER[0] - REGION, INNER[1] + 2 * REGION)
            hidden = h_one[0, around_rows, :].astype(F32)
            left = pltpu.roll(hidden, 1, 0).astype(BF)
            right = pltpu.roll(hidden, hidden.shape[0] - 1, 0).astype(BF)
            middle = hidden.astype(BF)
            gated = [
                (left * masks[0, around_rows, :], 0), (middle, 0), (right * masks[1, around_rows, :], 0),
                (left, 1), (middle, 1), (right, 1),
                (left * masks[2, around_rows, :], 2), (middle, 2), (right * masks[3, around_rows, :], 2),
            ]
            for tap, (value, dy) in enumerate(gated):
                column = value[dy * REGION : dy * REGION + INNER[1]]
                piece = fold_pair(mm_first(column, d_two), WIDTH, WIDTH)
                if tap < 4:
                    total[tap * 64 : tap * 64 + 64, :64] += piece
                elif tap > 4:
                    at = (tap - 5) * 64 + 32
                    total[at : at + 64, 64:] += piece
                else:
                    total[256:288, :64] += piece[:32]
                    total[0:32, 64:] += piece[32:]

        def second(j, c):
            start = pl.multiple_of(5 * REGION + j * 352, 32)
            rows = pl.ds(start, 352)
            d_hidden = mm(columns_at(shifted, start, 352), w_tap[b])
            d_first = (d_hidden * s_one[0, b, rows, :].astype(F32)).astype(BF)
            d_one[rows, :] = d_first
            d_three = region[rows, :].astype(F32) * s_three[0, b, rows, :].astype(F32)
            region[rows, :] = (d_three + mm(d_first, w_red[b])).astype(BF)
            return c

        lax.fori_loop(0, 2, second, 0)

        @pl.when(mine)
        def _():
            rows = pl.ds(*INNER)
            d_first = keep_inner(d_one[rows, :].astype(F32))
            piece = fold_pair(mm_first(a_own[0], d_first), CHANS, WIDTH)
            total[288:416, :64] += piece[:128]
            total[288:416, 64:] += piece[128:]
            grad_in[0] = inner_tile(region, 0)
            grad_in[1] = inner_tile(region, 1)

        return carry

    lax.fori_loop(0, 4, block, 0)

    @pl.when(pair == 1)
    def _():
        grads[...] = total[...].astype(BF)


SOURCES = 6


def run_kernel(body, scalars, sources, weights, blocked, outs, scratch):
    any_spec = pl.BlockSpec(memory_space=pl.ANY)

    def whole(item):
        return pl.BlockSpec(item.shape, lambda i, *_, n=len(item.shape): (0,) * n)

    def split(shape, count):
        return pl.BlockSpec(
            (count,) + tuple(shape[1:]), lambda i, *_, n=len(shape): (i,) + (0,) * (n - 1)
        )

    in_specs = (
        [any_spec] * len(sources)
        + [whole(item) for item in weights]
        + [split(item.shape, item.shape[0] // 2) for item in blocked]
    )
    out_specs = [whole(o) if fixed else split(o.shape, o.shape[0] // 2) for o, fixed in outs]
    return pl.pallas_call(
        body,
        grid_spec=pltpu.PrefetchScalarGridSpec(
            num_scalar_prefetch=len(scalars),
            grid=(2,),
            in_specs=in_specs,
            out_specs=out_specs,
            scratch_shapes=scratch,
        ),
        out_shape=[o for o, _ in outs],
        compiler_params=pltpu.CompilerParams(
            dimension_semantics=("arbitrary",), vmem_limit_bytes=VMEM_LIMIT
        ),
    )(*scalars, *sources, *weights, *blocked)


def shift(block, axes, distance):
    devices = range(lax.axis_size(axes))
    return lax.ppermute(block, axes, [(i, i + distance) for i in devices if i + distance in devices])


def other_core(block):
    return lax.ppermute(block, "core", [(0, 1), (1, 0)])


def gather_pool(own):
    close = jnp.concatenate([shift(own, TILE_AXES, 2), shift(own, TILE_AXES, -2)])
    far = jnp.concatenate([shift(own, TILE_AXES, 4), shift(own, TILE_AXES, -4)])
    return [own, close, far, other_core(own), other_core(close), other_core(far)]


def swap_chunks(parts, axes):
    return lax.all_to_all(parts, axes, 0, 0, tiled=True)


def sum_over_tiles(values):
    plane = ("y", "core")
    across = lax.axis_size(plane)
    deep = lax.axis_size("z")
    parts = values.reshape(across, -1)
    mine = jnp.sum(swap_chunks(parts, plane).astype(F32), axis=0)
    copies = jnp.broadcast_to(mine.astype(BF)[None], (deep,) + mine.shape)
    total = jnp.sum(swap_chunks(copies, "z").astype(F32), axis=0)
    copies = jnp.broadcast_to(total.astype(BF)[None], (across,) + total.shape)
    return swap_chunks(copies, plane).astype(F32).reshape(values.shape)


def split_float(value):
    high = value.astype(BF)
    low = (value - high.astype(F32)).astype(BF)
    return (high, low)


def gather_params(w_reduce, w_taps, w_expand, norm_scale, norm_shift):
    pieces = [w_reduce, w_taps, w_expand]
    for item in (norm_scale, norm_shift):
        pieces.extend(split_float(item))
    packed = jnp.concatenate([item.reshape(-1, 128) for item in pieces])
    every = lax.all_gather(packed, "section", axis=0, tiled=False)
    at = 0
    cut = []
    for item in pieces:
        rows = item.size // 128
        cut.append(every[:, at : at + rows].reshape((-1,) + item.shape[1:]))
        at += rows
    scale = cut[3].astype(F32) + cut[4].astype(F32)
    offset = cut[5].astype(F32) + cut[6].astype(F32)
    return (cut[0], cut[1], cut[2], scale, offset)


def twice(weights):
    zero = jnp.zeros_like(weights)
    return jnp.concatenate(
        [jnp.concatenate([weights, zero], axis=-1), jnp.concatenate([zero, weights], axis=-1)],
        axis=-2,
    )


def norm_rows(scale, offset):
    rows = []
    for low, high in ((0, 64), (64, 128), (128, 384)):
        for item in (scale, offset):
            part = jnp.concatenate([item[:, low:high]] * 2, axis=1)
            rows.append(jnp.pad(part, ((0, 0), (0, 512 - part.shape[1]))))
    rows.extend([jnp.zeros_like(rows[0])] * 2)
    return jnp.stack(rows, axis=1)


def on_device(
    features, out_cotangent, w_reduce, w_taps, w_expand, norm_scale, norm_shift, owner, neighbours
):
    here = lax.axis_index(TILE_AXES).astype(jnp.int32)
    section = lax.axis_index("section").astype(jnp.int32)
    slots = here * 4 + jnp.arange(4, dtype=jnp.int32)
    hit = owner[None, :] == slots[:, None]
    ids = jnp.sum(
        jnp.where(hit, jnp.arange(owner.shape[0], dtype=jnp.int32)[None, :], 0), axis=1
    )
    meta = jnp.concatenate([here[None], section[None], ids.astype(jnp.int32)])
    scalars = (meta, owner, neighbours.reshape(-1))

    sources = gather_pool(features)
    w_red, w_tap, w_exp, scale, offset = gather_params(
        w_reduce, w_taps, w_expand, norm_scale, norm_shift
    )
    taps = w_tap.reshape(4, TAPS, WIDTH, WIDTH)
    norms = norm_rows(scale, offset)
    ahead = (twice(w_red), twice(taps).reshape(4, TAPS * 128, 128), twice(w_exp), norms)
    back = (
        twice(w_red.swapaxes(1, 2)),
        twice(taps[:, ::-1].swapaxes(2, 3)).reshape(4, TAPS * 128, 128),
        twice(w_exp.swapaxes(1, 2)),
        norms,
    )
    waiting, *sources = lax.optimization_barrier((out_cotangent, *sources))
    later = gather_pool(waiting)

    def like(*shape):
        return jax.ShapeDtypeStruct(shape, BF)

    pool = [pltpu.VMEM((40, SIDE, SIDE, CHANS), BF), pltpu.SemaphoreType.DMA((SOURCES,))]
    region = pltpu.VMEM((PIXELS, 2 * CHANS), BF)
    narrow = (PIXELS, 2 * WIDTH)
    s_one, s_two, s_three, a_own, h_one, h_two, out = run_kernel(
        forward_kernel,
        scalars,
        sources,
        ahead,
        (),
        [
            (like(2, 4, *narrow), False),
            (like(2, 4, *narrow), False),
            (like(2, 4, PIXELS, 2 * CHANS), False),
            (like(2, INNER[1], 2 * CHANS), False),
            (like(2, *narrow), False),
            (like(2, *narrow), False),
            (like(4, SIDE, SIDE, CHANS), False),
        ],
        pool
        + [region, pltpu.VMEM(narrow, F32), pltpu.VMEM((4,) + narrow, BF), pltpu.VMEM((7,) + narrow, BF)],
    )
    grad_in, grads = run_kernel(
        backward_kernel,
        scalars,
        later,
        back,
        (s_one, s_two, s_three, a_own, h_one, h_two),
        [(like(4, SIDE, SIDE, CHANS), False), (like(544, 128), True)],
        pool
        + [
            region,
            pltpu.VMEM((4,) + narrow, BF),
            pltpu.VMEM((7,) + narrow, BF),
            pltpu.VMEM(narrow, BF),
            pltpu.VMEM((544, 128), F32),
        ],
    )
    total = sum_over_tiles(grads)
    g_taps = jnp.concatenate([total[:288, :64], total[:288, 64:]])
    g_reduce = jnp.concatenate([total[288:416, :64], total[288:416, 64:]])
    g_expand = jnp.concatenate([total[416:480], total[480:544]], axis=1)
    return (out[None], grad_in[None], g_reduce[None], g_taps[None], g_expand[None])


def fine_mesh(mesh):
    shape = (mesh.devices.shape[0], mesh.devices.shape[1] // 16, 8, 2)
    return Mesh(mesh.devices.reshape(shape), ("section",) + TILE_AXES)


def solution(mesh):
    tiles = P(TILE_AXES, None, None, None)
    owned = P("section", TILE_AXES, None, None, None)
    weights = P("section", None, None)
    return jax.shard_map(
        on_device,
        mesh=fine_mesh(mesh),
        in_specs=(
            tiles, tiles, weights, weights, weights, P("section", None), P("section", None), P(), P(),
        ),
        out_specs=(owned, owned, weights, weights, weights),
        check_vma=False,
    )
```

```python
import jax
import jax.numpy as jnp
from jax import lax
from jax.experimental import pallas as pl
from jax.experimental.pallas import tpu as pltpu
from jax.sharding import Mesh
from jax.sharding import PartitionSpec as P

TILE_AXES = ("z", "y", "core")
SIDE = 16
REGION = 32
HALO = 8
RIM = 4
PIXELS = REGION * REGION
WIDTH = 64
CHANS = 256
TAPS = 9
BF = jnp.bfloat16
F32 = jnp.float32
VMEM_LIMIT = 56 * 1024 * 1024


def mm(left, right):
    return jnp.dot(left, right, preferred_element_type=F32)


def mm_first(left, right):
    return lax.dot_general(left, right, (((0,), (0,)), ((), ())), preferred_element_type=F32)


def silu_parts(value):
    sig = 0.5 + 0.5 * jnp.tanh(0.5 * value)
    out = value * sig
    return (out, sig + out * (1.0 - sig))


def around(tile, owner, near):
    north, south = (near[tile * 4], near[tile * 4 + 1])
    west, east = (near[tile * 4 + 2], near[tile * 4 + 3])

    def step(first, way, second, other):
        one = jnp.where(first >= 0, near[jnp.maximum(first, 0) * 4 + way], -1)
        two = jnp.where(second >= 0, near[jnp.maximum(second, 0) * 4 + other], -1)
        return jnp.where(one >= 0, one, two)

    ids = [
        step(north, 2, west, 0), north, step(north, 3, east, 0),
        west, tile, east,
        step(south, 2, west, 1), south, step(south, 3, east, 1),
    ]
    found = [item >= 0 for item in ids]
    rows = [owner[jnp.maximum(item, 0)] for item in ids]
    return (rows, found)


def pool_place(row, here):
    device, slot = (row >> 2, row & 3)
    gap = (device >> 1) - (here >> 1)
    side = jnp.where(gap < 0, 0, 1)
    near = jnp.where(gap == 0, 0, 4 + 4 * side) + slot
    place = jnp.where(jnp.abs(gap) <= 1, near, 12 + 4 * side + slot)
    place = place + jnp.where((device & 1) == (here & 1), 0, 20)
    return jnp.clip(place, 0, 39)


def bands_of(halo):
    return (
        (HALO - halo, halo, 0, SIDE - halo),
        (HALO, SIDE, 3, 0),
        (HALO + SIDE, halo, 6, 0),
    )


def build_region(pool, region, lane, places, found, halo):
    for top, rows, first, start in bands_of(halo):
        parts = []
        for k in range(3):
            part = pool[places[first + k], pl.ds(start, rows)].astype(F32)
            part = jnp.where(found[first + k], part, 0.0)
            cut = (slice(HALO, SIDE), slice(0, SIDE), slice(0, HALO))[k]
            parts.append(part[:, cut, :])
        band = jnp.concatenate(parts, axis=1).reshape(rows * REGION, CHANS).astype(BF)
        region[pl.ds(top * REGION, rows * REGION), pl.ds(lane * CHANS, CHANS)] = band


def build_present(present, found_pair):
    for top, rows, first, _ in bands_of(HALO):
        shape = (rows * REGION, 2 * WIDTH)
        col = lax.broadcasted_iota(jnp.int32, shape, 0) % REGION
        lane = lax.broadcasted_iota(jnp.int32, shape, 1)
        sides = []
        for found in found_pair:
            flags = [jnp.where(found[first + k], 1.0, 0.0) for k in range(3)]
            sides.append(
                jnp.where(col < HALO, flags[0], jnp.where(col < HALO + SIDE, flags[1], flags[2]))
            )
        present[pl.ds(top * REGION, rows * REGION), :] = jnp.where(lane < WIDTH, sides[0], sides[1])


def build_masks(masks):
    shape = (PIXELS, 2 * WIDTH)
    pixel = lax.broadcasted_iota(jnp.int32, shape, 0)
    row, col = (pixel // REGION, pixel % REGION)
    low, high = (HALO, HALO + SIDE)
    west = (col == low) | (col == high)
    east = (col == low - 1) | (col == high - 1)
    above = (row == low - 1) | (row == high - 1)
    below = (row == low) | (row == high)
    for k, (across, along) in enumerate(
        ((above, west), (above, east), (below, west), (below, east))
    ):
        masks[k] = jnp.where(across & along, 0.0, 1.0).astype(BF)


def store_shifted(shifted, masks, start, value):
    count = value.shape[0]
    rows = pl.ds(start, count)
    left = pltpu.roll(value, 1, 0).astype(BF)
    right = pltpu.roll(value, count - 1, 0).astype(BF)
    shifted[0, rows, :] = left
    shifted[1, rows, :] = value.astype(BF)
    shifted[2, rows, :] = right
    shifted[3, rows, :] = left * masks[0, rows, :]
    shifted[4, rows, :] = right * masks[1, rows, :]
    shifted[5, rows, :] = left * masks[2, rows, :]
    shifted[6, rows, :] = right * masks[3, rows, :]


TAP_SOURCES = ((3, -1), (1, -1), (4, -1), (0, 0), (1, 0), (2, 0), (5, 1), (1, 1), (6, 1))


def columns_at(shifted, start, count):
    return jnp.concatenate(
        [shifted[k, pl.ds(start + dy * REGION, count), :] for k, dy in TAP_SOURCES], axis=1
    )


def run_copies(copies):
    for copy in copies:
        copy.start()
    for copy in copies:
        copy.wait()


def pool_copies(sources, pools, sems):
    feats, cots = ([], [])

    def add(group, source, target):
        sem = sems.at[len(feats) + len(cots)]
        group.append(pltpu.make_async_copy(source, target, sem))

    for core in range(2):
        at = 20 * core
        for source in sources[core][:3]:
            add(feats, source.at[pl.ds(0, 4)], pools[0].at[pl.ds(at, 4)])
            add(cots, source.at[pl.ds(4, 4)], pools[1].at[pl.ds(at, 4)])
            at += 4
        for source in sources[core][3:]:
            for k in range(4):
                add(feats, source.at[pl.ds(k * SIDE, SIDE)], pools[0].at[at])
                for end in range(2):
                    add(
                        cots,
                        source.at[pl.ds(4 * (SIDE + end * RIM) + k * RIM, RIM)],
                        pools[1].at[at, pl.ds(end * (SIDE - RIM), RIM)],
                    )
                at += 1
    return (feats, cots)


COPIES = 2 * (3 * 2 + 8 * 3)


def inner_tile(region, lane):
    value = region[pl.ds(HALO * REGION, SIDE * REGION), pl.ds(lane * CHANS, CHANS)].astype(F32)
    value = value.reshape(SIDE, REGION, CHANS)[:, HALO : HALO + SIDE, :]
    return value.astype(BF)


INNER = (HALO * REGION, SIDE * REGION)


def fold_pair(value, rows, cols):
    return value[:rows, :cols] + value[rows:, cols:]


def whole_kernel(meta, owner, near, *refs):
    sources, refs = ((refs[:5], refs[5:10]), refs[10:])
    (w_red, w_tap, w_exp, v_red, v_tap, v_exp, norms, out, grad_in, grads,
     feats, cots, sems, region, present, masks, shifted, s_one, s_two, s_three,
     a_own, h_one, h_two, d_one, total) = refs
    pair = pl.program_id(0)
    here, section = (meta[0], meta[1])
    copies = pool_copies(sources, (feats, cots), sems)

    @pl.when(pair == 0)
    def _():
        for group in copies:
            for copy in group:
                copy.start()
        build_masks(masks)
        total[...] = jnp.zeros_like(total)
        for copy in copies[0]:
            copy.wait()

    founds, places = ([], [])
    for lane in range(2):
        rows, found = around(meta[2 + pair * 2 + lane], owner, near)
        place = [pool_place(row, here) for row in rows]
        build_region(feats, region, lane, place, found, HALO)
        founds.append(found)
        places.append(place)
    build_present(present, founds)

    def ahead(b, carry):
        mine = b == section

        @pl.when(mine)
        def _():
            a_own[...] = region[pl.ds(*INNER), :]

        def front(j, c):
            start = pl.multiple_of(j * 256, 256)
            rows = pl.ds(start, 256)
            pre = mm(region[rows, :], w_red[b]) * norms[b, 0:1, :128] + norms[b, 1:2, :128]
            hidden, slope = silu_parts(pre)
            there = present[rows, :]
            s_one[b, rows, :] = (slope * there * norms[b, 0:1, :128]).astype(BF)
            store_shifted(shifted, masks, start, hidden * there)
            return c

        lax.fori_loop(0, 4, front, 0)

        def tail(j, c):
            start = pl.multiple_of(REGION + j * 320, 32)
            rows = pl.ds(start, 320)
            pre = mm(columns_at(shifted, start, 320), w_tap[b])
            pre = pre * norms[b, 2:3, :128] + norms[b, 3:4, :128]
            hidden, slope = silu_parts(pre)
            s_two[b, rows, :] = (slope * norms[b, 2:3, :128]).astype(BF)
            hidden = hidden.astype(BF)

            @pl.when(mine)
            def _():
                h_two[rows, :] = hidden

            pre = (
                region[rows, :].astype(F32)
                + mm(hidden, w_exp[b]) * norms[b, 4:5, :]
                + norms[b, 5:6, :]
            )
            value, slope = silu_parts(pre)
            region[rows, :] = value.astype(BF)
            s_three[b, rows, :] = slope.astype(BF)
            return c

        lax.fori_loop(0, 3, tail, 0)

        @pl.when(mine)
        def _():
            h_one[...] = shifted[1]
            out[0] = inner_tile(region, 0)
            out[1] = inner_tile(region, 1)

        return carry

    lax.fori_loop(0, 4, ahead, 0)

    @pl.when(pair == 0)
    def _():
        for copy in copies[1]:
            copy.wait()

    for lane in range(2):
        build_region(cots, region, lane, places[lane], founds[lane], RIM)

    def keep_inner(value):
        col = lax.broadcasted_iota(jnp.int32, value.shape, 0) % REGION
        return jnp.where((col >= HALO) & (col < HALO + SIDE), value, 0.0).astype(BF)

    def back(step, carry):
        b = 3 - step
        mine = b == section

        def first(j, c):
            start = pl.multiple_of(4 * REGION + j * 256, 128)
            rows = pl.ds(start, 256)
            d_three = region[rows, :].astype(F32) * s_three[b, rows, :].astype(F32)
            e_three = (d_three * norms[b, 4:5, :]).astype(BF)
            d_two = mm(e_three, v_exp[b]) * s_two[b, rows, :].astype(F32)
            store_shifted(shifted, masks, start, d_two)
            return c

        lax.fori_loop(0, 3, first, 0)

        @pl.when(mine)
        def _():
            rows = pl.ds(*INNER)
            d_three = region[rows, :].astype(F32) * s_three[b, rows, :].astype(F32)
            e_three = keep_inner(d_three * norms[b, 4:5, :])
            total_e = fold_pair(mm_first(h_two[rows, :], e_three), WIDTH, CHANS)
            total[416:480, :] += total_e[:, :128]
            total[480:544, :] += total_e[:, 128:]
            d_two = keep_inner(shifted[1, rows, :].astype(F32))
            around_rows = pl.ds(INNER[0] - REGION, INNER[1] + 2 * REGION)
            hidden = h_one[around_rows, :].astype(F32)
            left = pltpu.roll(hidden, 1, 0).astype(BF)
            right = pltpu.roll(hidden, hidden.shape[0] - 1, 0).astype(BF)
            middle = hidden.astype(BF)
            gated = [
                (left * masks[0, around_rows, :], 0), (middle, 0), (right * masks[1, around_rows, :], 0),
                (left, 1), (middle, 1), (right, 1),
                (left * masks[2, around_rows, :], 2), (middle, 2), (right * masks[3, around_rows, :], 2),
            ]
            for tap, (value, dy) in enumerate(gated):
                column = value[dy * REGION : dy * REGION + INNER[1]]
                piece = fold_pair(mm_first(column, d_two), WIDTH, WIDTH)
                if tap < 4:
                    total[tap * 64 : tap * 64 + 64, :64] += piece
                elif tap > 4:
                    at = (tap - 5) * 64 + 32
                    total[at : at + 64, 64:] += piece
                else:
                    total[256:288, :64] += piece[:32]
                    total[0:32, 64:] += piece[32:]

        def second(j, c):
            start = pl.multiple_of(5 * REGION + j * 352, 32)
            rows = pl.ds(start, 352)
            d_hidden = mm(columns_at(shifted, start, 352), v_tap[b])
            d_first = (d_hidden * s_one[b, rows, :].astype(F32)).astype(BF)
            d_one[rows, :] = d_first
            d_three = region[rows, :].astype(F32) * s_three[b, rows, :].astype(F32)
            region[rows, :] = (d_three + mm(d_first, v_red[b])).astype(BF)
            return c

        lax.fori_loop(0, 2, second, 0)

        @pl.when(mine)
        def _():
            rows = pl.ds(*INNER)
            d_first = keep_inner(d_one[rows, :].astype(F32))
            piece = fold_pair(mm_first(a_own[...], d_first), CHANS, WIDTH)
            total[288:416, :64] += piece[:128]
            total[288:416, 64:] += piece[128:]
            grad_in[0] = inner_tile(region, 0)
            grad_in[1] = inner_tile(region, 1)

        return carry

    lax.fori_loop(0, 4, back, 0)

    @pl.when(pair == 1)
    def _():
        grads[...] = total[...].astype(BF)


def run_kernel(scalars, sources, weights):
    def whole(item):
        return pl.BlockSpec(item.shape, lambda i, *_, n=len(item.shape): (0,) * n)

    tiles = jax.ShapeDtypeStruct((4, SIDE, SIDE, CHANS), BF)
    grads = jax.ShapeDtypeStruct((640, 128), BF)
    pair = pl.BlockSpec((2, SIDE, SIDE, CHANS), lambda i, *_: (i, 0, 0, 0))
    narrow = (PIXELS, 2 * WIDTH)
    pool = pltpu.VMEM((40, SIDE, SIDE, CHANS), BF)
    wide = (PIXELS, 2 * CHANS)
    return pl.pallas_call(
        whole_kernel,
        grid_spec=pltpu.PrefetchScalarGridSpec(
            num_scalar_prefetch=len(scalars),
            grid=(2,),
            in_specs=[pl.BlockSpec(memory_space=pl.ANY)] * len(sources)
            + [whole(item) for item in weights],
            out_specs=[pair, pair, whole(grads)],
            scratch_shapes=[
                pool,
                pool,
                pltpu.SemaphoreType.DMA((COPIES,)),
                pltpu.VMEM(wide, BF),
                pltpu.VMEM(narrow, F32),
                pltpu.VMEM((4,) + narrow, BF),
                pltpu.VMEM((7,) + narrow, BF),
                pltpu.VMEM((4,) + narrow, BF),
                pltpu.VMEM((4,) + narrow, BF),
                pltpu.VMEM((4,) + wide, BF),
                pltpu.VMEM((INNER[1], 2 * CHANS), BF),
                pltpu.VMEM(narrow, BF),
                pltpu.VMEM(narrow, BF),
                pltpu.VMEM(narrow, BF),
                pltpu.VMEM((640, 128), F32),
            ],
        ),
        out_shape=[tiles, tiles, grads],
        compiler_params=pltpu.CompilerParams(
            dimension_semantics=("arbitrary",), vmem_limit_bytes=VMEM_LIMIT
        ),
    )(*scalars, *sources, *weights)


def shift(block, axes, distance):
    devices = range(lax.axis_size(axes))
    return lax.ppermute(block, axes, [(i, i + distance) for i in devices if i + distance in devices])


def other_core(block):
    return lax.ppermute(block, "core", [(0, 1), (1, 0)])


def trimmed(both):
    ends = (both[4:, :RIM], both[4:, SIDE - RIM :])
    return jnp.concatenate([item.reshape(-1, SIDE, CHANS) for item in (both[:4], *ends)])


def exchange(features, cotangent):
    both = jnp.concatenate([features, cotangent])
    column = [both]
    for distance in (2, -2):
        column.append(shift(both, TILE_AXES, distance))
    for k, distance in ((1, 2), (2, -2)):
        column.append(shift(trimmed(column[k]), TILE_AXES, distance))
    return column + [other_core(item) for item in column]


def swap_chunks(parts, axes):
    return lax.all_to_all(parts, axes, 0, 0, tiled=True)


def sum_over_tiles(values):
    plane = ("y", "core")
    across = lax.axis_size(plane)
    rows = values.shape[0] // across
    got = swap_chunks(values, plane).reshape(across, rows, 128)
    mine = jnp.sum(got.astype(F32), axis=0).astype(BF)
    got = swap_chunks(jnp.tile(mine, (lax.axis_size("z"), 1)), "z").reshape(-1, rows, 128)
    total = jnp.sum(got.astype(F32), axis=0).astype(BF)
    return swap_chunks(jnp.tile(total, (across, 1)), plane).astype(F32)


def split_float(value):
    high = value.astype(BF)
    low = (value - high.astype(F32)).astype(BF)
    return (high, low)


def gather_params(w_reduce, w_taps, w_expand, norm_scale, norm_shift):
    pieces = [w_reduce, w_taps, w_expand]
    for item in (norm_scale, norm_shift):
        pieces.extend(split_float(item))
    packed = jnp.concatenate([item.reshape(-1, 128) for item in pieces])
    every = lax.all_gather(packed, "section", axis=0, tiled=False)
    at = 0
    cut = []
    for item in pieces:
        rows = item.size // 128
        cut.append(every[:, at : at + rows].reshape((-1,) + item.shape[1:]))
        at += rows
    scale = cut[3].astype(F32) + cut[4].astype(F32)
    offset = cut[5].astype(F32) + cut[6].astype(F32)
    return (cut[0], cut[1], cut[2], scale, offset)


def twice(weights):
    zero = jnp.zeros_like(weights)
    return jnp.concatenate(
        [jnp.concatenate([weights, zero], axis=-1), jnp.concatenate([zero, weights], axis=-1)],
        axis=-2,
    )


def norm_rows(scale, offset):
    rows = []
    for low, high in ((0, 64), (64, 128), (128, 384)):
        for item in (scale, offset):
            part = jnp.concatenate([item[:, low:high]] * 2, axis=1)
            rows.append(jnp.pad(part, ((0, 0), (0, 512 - part.shape[1]))))
    rows.extend([jnp.zeros_like(rows[0])] * 2)
    return jnp.stack(rows, axis=1)


def on_device(
    features, out_cotangent, w_reduce, w_taps, w_expand, norm_scale, norm_shift, owner, neighbours
):
    here = lax.axis_index(TILE_AXES).astype(jnp.int32)
    section = lax.axis_index("section").astype(jnp.int32)
    slots = here * 4 + jnp.arange(4, dtype=jnp.int32)
    hit = owner[None, :] == slots[:, None]
    ids = jnp.sum(
        jnp.where(hit, jnp.arange(owner.shape[0], dtype=jnp.int32)[None, :], 0), axis=1
    )
    meta = jnp.concatenate([here[None], section[None], ids.astype(jnp.int32)])
    scalars = (meta, owner, neighbours.reshape(-1))

    sources = exchange(features, out_cotangent)
    w_red, w_tap, w_exp, scale, offset = gather_params(
        w_reduce, w_taps, w_expand, norm_scale, norm_shift
    )
    taps = w_tap.reshape(4, TAPS, WIDTH, WIDTH)
    weights = (
        twice(w_red),
        twice(taps).reshape(4, TAPS * 128, 128),
        twice(w_exp),
        twice(w_red.swapaxes(1, 2)),
        twice(taps[:, ::-1].swapaxes(2, 3)).reshape(4, TAPS * 128, 128),
        twice(w_exp.swapaxes(1, 2)),
        norm_rows(scale, offset),
    )
    out, grad_in, grads = run_kernel(scalars, sources, weights)
    total = sum_over_tiles(grads)
    g_taps = jnp.concatenate([total[:288, :64], total[:288, 64:]])
    g_reduce = jnp.concatenate([total[288:416, :64], total[288:416, 64:]])
    g_expand = jnp.concatenate([total[416:480], total[480:544]], axis=1)
    return (out[None], grad_in[None], g_reduce[None], g_taps[None], g_expand[None])


def fine_mesh(mesh):
    shape = (mesh.devices.shape[0], mesh.devices.shape[1] // 16, 8, 2)
    return Mesh(mesh.devices.reshape(shape), ("section",) + TILE_AXES)


def solution(mesh):
    tiles = P(TILE_AXES, None, None, None)
    owned = P("section", TILE_AXES, None, None, None)
    weights = P("section", None, None)
    return jax.shard_map(
        on_device,
        mesh=fine_mesh(mesh),
        in_specs=(
            tiles, tiles, weights, weights, weights, P("section", None), P("section", None), P(), P(),
        ),
        out_specs=(owned, owned, weights, weights, weights),
        check_vma=False,
    )
```

```python
import jax
import jax.numpy as jnp
from jax import lax
from jax.experimental import pallas as pl
from jax.experimental.pallas import tpu as pltpu
from jax.sharding import Mesh
from jax.sharding import PartitionSpec as P

TILE_AXES = ("z", "y", "core")
SIDE = 16
REGION = 32
HALO = 8
RIM = 4
PIXELS = REGION * REGION
WIDTH = 64
CHANS = 256
BF = jnp.bfloat16
F32 = jnp.float32
VMEM_LIMIT = 56 * 1024 * 1024


def mm(left, right):
    return jnp.dot(left, right, preferred_element_type=F32)


def mm_first(left, right):
    return lax.dot_general(left, right, (((0,), (0,)), ((), ())), preferred_element_type=F32)


def silu_parts(value):
    sig = 0.5 + 0.5 * jnp.tanh(0.5 * value)
    out = value * sig
    return (out, sig + out * (1.0 - sig))


def around(tile, owner, near):
    north, south = (near[tile * 4], near[tile * 4 + 1])
    west, east = (near[tile * 4 + 2], near[tile * 4 + 3])

    def step(first, way, second, other):
        one = jnp.where(first >= 0, near[jnp.maximum(first, 0) * 4 + way], -1)
        two = jnp.where(second >= 0, near[jnp.maximum(second, 0) * 4 + other], -1)
        return jnp.where(one >= 0, one, two)

    ids = [
        step(north, 2, west, 0), north, step(north, 3, east, 0),
        west, tile, east,
        step(south, 2, west, 1), south, step(south, 3, east, 1),
    ]
    found = [item >= 0 for item in ids]
    rows = [owner[jnp.maximum(item, 0)] for item in ids]
    return (rows, found)


def pool_place(row, here):
    device, slot = (row >> 2, row & 3)
    gap = (device >> 1) - (here >> 1)
    side = jnp.where(gap < 0, 0, 1)
    near = jnp.where(gap == 0, 0, 4 + 4 * side) + slot
    place = jnp.where(jnp.abs(gap) <= 1, near, 12 + 4 * side + slot)
    place = place + jnp.where((device & 1) == (here & 1), 0, 20)
    return jnp.clip(place, 0, 39)


def bands_of(halo):
    return (
        (HALO - halo, halo, 0, SIDE - halo),
        (HALO, SIDE, 3, 0),
        (HALO + SIDE, halo, 6, 0),
    )


def build_region(pool, region, lane, places, found, halo):
    for top, rows, first, start in bands_of(halo):
        parts = []
        for k in range(3):
            part = pool[places[first + k], pl.ds(start, rows)].astype(F32)
            part = jnp.where(found[first + k], part, 0.0)
            cut = (slice(HALO, SIDE), slice(0, SIDE), slice(0, HALO))[k]
            parts.append(part[:, cut, :])
        band = jnp.concatenate(parts, axis=1).reshape(rows * REGION, CHANS).astype(BF)
        region[pl.ds(top * REGION, rows * REGION), pl.ds(lane * CHANS, CHANS)] = band


def build_present(present, found_pair):
    for top, rows, first, _ in bands_of(HALO):
        shape = (rows * REGION, 2 * WIDTH)
        col = lax.broadcasted_iota(jnp.int32, shape, 0) % REGION
        lane = lax.broadcasted_iota(jnp.int32, shape, 1)
        sides = []
        for found in found_pair:
            flags = [jnp.where(found[first + k], 1.0, 0.0) for k in range(3)]
            sides.append(
                jnp.where(col < HALO, flags[0], jnp.where(col < HALO + SIDE, flags[1], flags[2]))
            )
        present[pl.ds(top * REGION, rows * REGION), :] = jnp.where(lane < WIDTH, sides[0], sides[1])


def build_masks(masks):
    shape = (PIXELS, 2 * WIDTH)
    pixel = lax.broadcasted_iota(jnp.int32, shape, 0)
    row, col = (pixel // REGION, pixel % REGION)
    low, high = (HALO, HALO + SIDE)
    west = (col == low) | (col == high)
    east = (col == low - 1) | (col == high - 1)
    above = (row == low - 1) | (row == high - 1)
    below = (row == low) | (row == high)
    for k, (across, along) in enumerate(
        ((above, west), (above, east), (below, west), (below, east))
    ):
        masks[k] = jnp.where(across & along, 0.0, 1.0).astype(BF)


def low_lanes(rows):
    return lax.broadcasted_iota(jnp.int32, (rows, 2 * WIDTH), 1) < WIDTH


def build_gates(gates):
    col = lax.broadcasted_iota(jnp.int32, (4 * REGION, 2 * WIDTH), 0) % REGION
    west = (col == HALO) | (col == HALO + SIDE)
    east = (col == HALO - 1) | (col == HALO + SIDE - 1)
    left = jnp.where(west & low_lanes(4 * REGION), 0.0, 1.0).astype(BF)
    gates[:, 0:128] = left
    gates[:, 128:256] = left
    gates[:, 256:384] = jnp.where(east, 0.0, 1.0).astype(BF)


def store_shifted(stack, center, start, value):
    count = value.shape[0]
    rows = pl.ds(start, count)
    low = low_lanes(count)
    other = pltpu.roll(value, WIDTH, 1)
    left = pltpu.roll(value, 1, 0)
    other_left = pltpu.roll(other, 1, 0)
    right = pltpu.roll(value, count - 1, 0)
    stack[rows, 0:128] = jnp.where(low, left, other).astype(BF)
    stack[rows, 128:256] = jnp.where(low, other_left, value).astype(BF)
    stack[rows, 256:384] = right.astype(BF)
    center[rows, :] = value.astype(BF)


def row_products(first, second, third, weights):
    one = mm(jnp.concatenate([first, third], axis=1), weights[0])
    two = mm(jnp.concatenate([second, third], axis=1), weights[1])
    low = low_lanes(first.shape[0])
    above = jnp.where(low, one[:, :128], two[:, :128])
    level = pltpu.roll(jnp.where(low, two[:, :128], one[:, :128]), WIDTH, 1)
    return (above, level, one[:, 128:] + two[:, 128:])


def convolve(stack, gates, products, start, count, weights):
    rows = pl.ds(start, count)
    parts = row_products(stack[rows, 0:128], stack[rows, 128:256], stack[rows, 256:384], weights)
    for k in range(3):
        products[k, rows, :] = parts[k]
    upper, lower = ((HALO - 1) * REGION, (HALO + SIDE - 1) * REGION)
    pair = 2 * REGION
    edge = jnp.concatenate([stack[pl.ds(upper, pair), :], stack[pl.ds(lower, pair), :]])
    edge = edge * gates[...]
    above, _, below = row_products(edge[:, 0:128], edge[:, 128:256], edge[:, 256:384], weights)
    for k, at in enumerate((upper, lower)):
        products[0, pl.ds(at, REGION), :] = above[k * pair : k * pair + REGION]
        products[2, pl.ds(at + REGION, REGION), :] = below[k * pair + REGION : (k + 1) * pair]
    inner = pl.ds(start + REGION, count - pair)
    return (
        products[0, pl.ds(start, count - pair), :]
        + products[1, inner, :]
        + products[2, pl.ds(start + pair, count - pair), :]
    )


def pool_copies(sources, pools, sems):
    feats, cots = ([], [])

    def add(group, source, target):
        sem = sems.at[len(feats) + len(cots)]
        group.append(pltpu.make_async_copy(source, target, sem))

    for core in range(2):
        at = 20 * core
        for source in sources[core][:3]:
            add(feats, source.at[pl.ds(0, 4)], pools[0].at[pl.ds(at, 4)])
            add(cots, source.at[pl.ds(4, 4)], pools[1].at[pl.ds(at, 4)])
            at += 4
        for source in sources[core][3:]:
            for k in range(4):
                add(feats, source.at[pl.ds(k * SIDE, SIDE)], pools[0].at[at])
                for end in range(2):
                    add(
                        cots,
                        source.at[pl.ds(4 * (SIDE + end * RIM) + k * RIM, RIM)],
                        pools[1].at[at, pl.ds(end * (SIDE - RIM), RIM)],
                    )
                at += 1
    return (feats, cots)


COPIES = 2 * (3 * 2 + 8 * 3)


def inner_tile(region, lane):
    value = region[pl.ds(HALO * REGION, SIDE * REGION), pl.ds(lane * CHANS, CHANS)].astype(F32)
    value = value.reshape(SIDE, REGION, CHANS)[:, HALO : HALO + SIDE, :]
    return value.astype(BF)


INNER = (HALO * REGION, SIDE * REGION)


def fold_pair(value, rows, cols):
    return value[:rows, :cols] + value[rows:, cols:]


def whole_kernel(meta, owner, near, *refs):
    sources, refs = ((refs[:5], refs[5:10]), refs[10:])
    (w_red, w_tap, w_exp, v_red, v_tap, v_exp, norms, out, grad_in, grads,
     feats, cots, sems, region, present, masks, gates, stack, center, products, s_one, s_two, s_three,
     a_own, h_one, h_two, d_one, total) = refs
    pair = pl.program_id(0)
    here, section = (meta[0], meta[1])
    copies = pool_copies(sources, (feats, cots), sems)

    @pl.when(pair == 0)
    def _():
        for group in copies:
            for copy in group:
                copy.start()
        build_masks(masks)
        build_gates(gates)
        total[...] = jnp.zeros_like(total)
        for copy in copies[0]:
            copy.wait()

    founds, places = ([], [])
    for lane in range(2):
        rows, found = around(meta[2 + pair * 2 + lane], owner, near)
        place = [pool_place(row, here) for row in rows]
        build_region(feats, region, lane, place, found, HALO)
        founds.append(found)
        places.append(place)
    build_present(present, founds)

    def ahead(b, carry):
        mine = b == section

        @pl.when(mine)
        def _():
            a_own[...] = region[pl.ds(*INNER), :]

        def front():
            start, count = (0, PIXELS)
            rows = pl.ds(start, count)
            pre = mm(region[rows, :], w_red[b]) * norms[b, 0:1, :128] + norms[b, 1:2, :128]
            hidden, slope = silu_parts(pre)
            there = present[rows, :]
            s_one[b, rows, :] = (slope * there * norms[b, 0:1, :128]).astype(BF)
            store_shifted(stack, center, start, hidden * there)

        front()

        def tail():
            start, count = (REGION, PIXELS - 2 * REGION)
            rows = pl.ds(start, count)
            pre = convolve(stack, gates, products, 0, PIXELS, w_tap[b])
            pre = pre * norms[b, 2:3, :128] + norms[b, 3:4, :128]
            hidden, slope = silu_parts(pre)
            s_two[b, rows, :] = (slope * norms[b, 2:3, :128]).astype(BF)
            hidden = hidden.astype(BF)

            @pl.when(mine)
            def _():
                h_two[rows, :] = hidden

            pre = (
                region[rows, :].astype(F32)
                + mm(hidden, w_exp[b]) * norms[b, 4:5, :]
                + norms[b, 5:6, :]
            )
            value, slope = silu_parts(pre)
            region[rows, :] = value.astype(BF)
            s_three[b, rows, :] = slope.astype(BF)

        tail()

        @pl.when(mine)
        def _():
            h_one[...] = center[...]
            out[0] = inner_tile(region, 0)
            out[1] = inner_tile(region, 1)

        return carry

    lax.fori_loop(0, 4, ahead, 0)

    @pl.when(pair == 0)
    def _():
        for copy in copies[1]:
            copy.wait()

    for lane in range(2):
        build_region(cots, region, lane, places[lane], founds[lane], RIM)

    def keep_inner(value):
        col = lax.broadcasted_iota(jnp.int32, value.shape, 0) % REGION
        return jnp.where((col >= HALO) & (col < HALO + SIDE), value, 0.0).astype(BF)

    def back(step, carry):
        b = 3 - step
        mine = b == section

        def first():
            start, count = (4 * REGION, PIXELS - 8 * REGION)
            rows = pl.ds(start, count)
            d_three = region[rows, :].astype(F32) * s_three[b, rows, :].astype(F32)
            e_three = (d_three * norms[b, 4:5, :]).astype(BF)
            d_two = mm(e_three, v_exp[b]) * s_two[b, rows, :].astype(F32)
            store_shifted(stack, center, start, d_two)

        first()

        @pl.when(mine)
        def _():
            rows = pl.ds(*INNER)
            d_three = region[rows, :].astype(F32) * s_three[b, rows, :].astype(F32)
            e_three = keep_inner(d_three * norms[b, 4:5, :])
            total_e = fold_pair(mm_first(h_two[rows, :], e_three), WIDTH, CHANS)
            total[416:480, :] += total_e[:, :128]
            total[480:544, :] += total_e[:, 128:]
            d_two = keep_inner(center[rows, :].astype(F32))
            around_rows = pl.ds(INNER[0] - REGION, INNER[1] + 2 * REGION)
            hidden = h_one[around_rows, :].astype(F32)
            left = pltpu.roll(hidden, 1, 0).astype(BF)
            right = pltpu.roll(hidden, hidden.shape[0] - 1, 0).astype(BF)
            middle = hidden.astype(BF)
            gated = [
                (left * masks[0, around_rows, :], 0), (middle, 0), (right * masks[1, around_rows, :], 0),
                (left, 1), (middle, 1), (right, 1),
                (left * masks[2, around_rows, :], 2), (middle, 2), (right * masks[3, around_rows, :], 2),
            ]
            for tap, (value, dy) in enumerate(gated):
                column = value[dy * REGION : dy * REGION + INNER[1]]
                piece = fold_pair(mm_first(column, d_two), WIDTH, WIDTH)
                if tap < 4:
                    total[tap * 64 : tap * 64 + 64, :64] += piece
                elif tap > 4:
                    at = (tap - 5) * 64 + 32
                    total[at : at + 64, 64:] += piece
                else:
                    total[256:288, :64] += piece[:32]
                    total[0:32, 64:] += piece[32:]

        def second():
            start, count = (5 * REGION, PIXELS - 10 * REGION)
            rows = pl.ds(start, count)
            d_hidden = convolve(
                stack, gates, products, 4 * REGION, PIXELS - 8 * REGION, v_tap[b]
            )
            d_first = (d_hidden * s_one[b, rows, :].astype(F32)).astype(BF)
            d_one[rows, :] = d_first
            d_three = region[rows, :].astype(F32) * s_three[b, rows, :].astype(F32)
            region[rows, :] = (d_three + mm(d_first, v_red[b])).astype(BF)

        second()

        @pl.when(mine)
        def _():
            rows = pl.ds(*INNER)
            d_first = keep_inner(d_one[rows, :].astype(F32))
            piece = fold_pair(mm_first(a_own[...], d_first), CHANS, WIDTH)
            total[288:416, :64] += piece[:128]
            total[288:416, 64:] += piece[128:]
            grad_in[0] = inner_tile(region, 0)
            grad_in[1] = inner_tile(region, 1)

        return carry

    lax.fori_loop(0, 4, back, 0)

    @pl.when(pair == 1)
    def _():
        grads[...] = total[...].astype(BF)


def run_kernel(scalars, sources, weights):
    def whole(item):
        return pl.BlockSpec(item.shape, lambda i, *_, n=len(item.shape): (0,) * n)

    tiles = jax.ShapeDtypeStruct((4, SIDE, SIDE, CHANS), BF)
    grads = jax.ShapeDtypeStruct((640, 128), BF)
    pair = pl.BlockSpec((2, SIDE, SIDE, CHANS), lambda i, *_: (i, 0, 0, 0))
    narrow = (PIXELS, 2 * WIDTH)
    pool = pltpu.VMEM((40, SIDE, SIDE, CHANS), BF)
    wide = (PIXELS, 2 * CHANS)
    return pl.pallas_call(
        whole_kernel,
        grid_spec=pltpu.PrefetchScalarGridSpec(
            num_scalar_prefetch=len(scalars),
            grid=(2,),
            in_specs=[pl.BlockSpec(memory_space=pl.ANY)] * len(sources)
            + [whole(item) for item in weights],
            out_specs=[pair, pair, whole(grads)],
            scratch_shapes=[
                pool,
                pool,
                pltpu.SemaphoreType.DMA((COPIES,)),
                pltpu.VMEM(wide, BF),
                pltpu.VMEM(narrow, F32),
                pltpu.VMEM((4,) + narrow, BF),
                pltpu.VMEM((4 * REGION, 6 * WIDTH), BF),
                pltpu.VMEM((PIXELS, 6 * WIDTH), BF),
                pltpu.VMEM(narrow, BF),
                pltpu.VMEM((3,) + narrow, F32),
                pltpu.VMEM((4,) + narrow, BF),
                pltpu.VMEM((4,) + narrow, BF),
                pltpu.VMEM((4,) + wide, BF),
                pltpu.VMEM((INNER[1], 2 * CHANS), BF),
                pltpu.VMEM(narrow, BF),
                pltpu.VMEM(narrow, BF),
                pltpu.VMEM(narrow, BF),
                pltpu.VMEM((640, 128), F32),
            ],
        ),
        out_shape=[tiles, tiles, grads],
        compiler_params=pltpu.CompilerParams(
            dimension_semantics=("arbitrary",), vmem_limit_bytes=VMEM_LIMIT
        ),
    )(*scalars, *sources, *weights)


def shift(block, axes, distance):
    devices = range(lax.axis_size(axes))
    return lax.ppermute(block, axes, [(i, i + distance) for i in devices if i + distance in devices])


def other_core(block):
    return lax.ppermute(block, "core", [(0, 1), (1, 0)])


def trimmed(both):
    ends = (both[4:, :RIM], both[4:, SIDE - RIM :])
    return jnp.concatenate([item.reshape(-1, SIDE, CHANS) for item in (both[:4], *ends)])


def exchange(features, cotangent):
    both = jnp.concatenate([features, cotangent])
    column = [both]
    for distance in (2, -2):
        column.append(shift(both, TILE_AXES, distance))
    for k, distance in ((1, 2), (2, -2)):
        column.append(shift(trimmed(column[k]), TILE_AXES, distance))
    return column + [other_core(item) for item in column]


def swap_chunks(parts, axes):
    return lax.all_to_all(parts, axes, 0, 0, tiled=True)


def sum_over_tiles(values):
    plane = ("y", "core")
    across = lax.axis_size(plane)
    rows = values.shape[0] // across
    got = swap_chunks(values, plane).reshape(across, rows, 128)
    mine = jnp.sum(got.astype(F32), axis=0).astype(BF)
    got = swap_chunks(jnp.tile(mine, (lax.axis_size("z"), 1)), "z").reshape(-1, rows, 128)
    total = jnp.sum(got.astype(F32), axis=0).astype(BF)
    return swap_chunks(jnp.tile(total, (across, 1)), plane).astype(F32)


def split_float(value):
    high = value.astype(BF)
    low = (value - high.astype(F32)).astype(BF)
    return (high, low)


def gather_params(w_reduce, w_taps, w_expand, norm_scale, norm_shift):
    pieces = [w_reduce, w_taps, w_expand]
    for item in (norm_scale, norm_shift):
        pieces.extend(split_float(item))
    packed = jnp.concatenate([item.reshape(-1, 128) for item in pieces])
    every = lax.all_gather(packed, "section", axis=0, tiled=False)
    at = 0
    cut = []
    for item in pieces:
        rows = item.size // 128
        cut.append(every[:, at : at + rows].reshape((-1,) + item.shape[1:]))
        at += rows
    scale = cut[3].astype(F32) + cut[4].astype(F32)
    offset = cut[5].astype(F32) + cut[6].astype(F32)
    return (cut[0], cut[1], cut[2], scale, offset)


def twice(weights):
    zero = jnp.zeros_like(weights)
    return jnp.concatenate(
        [jnp.concatenate([weights, zero], axis=-1), jnp.concatenate([zero, weights], axis=-1)],
        axis=-2,
    )


def tap_pair(taps):
    blank = jnp.zeros_like(taps[:, 0, 0])

    def grid(rows, cols):
        lines = []
        for dx in rows:
            line = [blank if None in (dx, dy) else taps[:, dy, dx] for dy in cols]
            lines.append(jnp.concatenate(line, axis=2))
        return jnp.concatenate(lines, axis=1)

    return jnp.stack([grid((0, 1, 2, None), (0, 1, 2, None)), grid((0, 1, None, 2), (1, 0, None, 2))], axis=1)


def norm_rows(scale, offset):
    rows = []
    for low, high in ((0, 64), (64, 128), (128, 384)):
        for item in (scale, offset):
            part = jnp.concatenate([item[:, low:high]] * 2, axis=1)
            rows.append(jnp.pad(part, ((0, 0), (0, 512 - part.shape[1]))))
    rows.extend([jnp.zeros_like(rows[0])] * 2)
    return jnp.stack(rows, axis=1)


def on_device(
    features, out_cotangent, w_reduce, w_taps, w_expand, norm_scale, norm_shift, owner, neighbours
):
    here = lax.axis_index(TILE_AXES).astype(jnp.int32)
    section = lax.axis_index("section").astype(jnp.int32)
    slots = here * 4 + jnp.arange(4, dtype=jnp.int32)
    hit = owner[None, :] == slots[:, None]
    ids = jnp.sum(
        jnp.where(hit, jnp.arange(owner.shape[0], dtype=jnp.int32)[None, :], 0), axis=1
    )
    meta = jnp.concatenate([here[None], section[None], ids.astype(jnp.int32)])
    scalars = (meta, owner, neighbours.reshape(-1))

    sources = exchange(features, out_cotangent)
    w_red, w_tap, w_exp, scale, offset = gather_params(
        w_reduce, w_taps, w_expand, norm_scale, norm_shift
    )
    taps = w_tap.reshape(4, 3, 3, WIDTH, WIDTH)
    turned = taps[:, ::-1, ::-1].swapaxes(3, 4)
    weights = (
        twice(w_red),
        tap_pair(taps),
        twice(w_exp),
        twice(w_red.swapaxes(1, 2)),
        tap_pair(turned),
        twice(w_exp.swapaxes(1, 2)),
        norm_rows(scale, offset),
    )
    out, grad_in, grads = run_kernel(scalars, sources, weights)
    total = sum_over_tiles(grads)
    g_taps = jnp.concatenate([total[:288, :64], total[:288, 64:]])
    g_reduce = jnp.concatenate([total[288:416, :64], total[288:416, 64:]])
    g_expand = jnp.concatenate([total[416:480], total[480:544]], axis=1)
    return (out[None], grad_in[None], g_reduce[None], g_taps[None], g_expand[None])


def fine_mesh(mesh):
    shape = (mesh.devices.shape[0], mesh.devices.shape[1] // 16, 8, 2)
    return Mesh(mesh.devices.reshape(shape), ("section",) + TILE_AXES)


def solution(mesh):
    tiles = P(TILE_AXES, None, None, None)
    owned = P("section", TILE_AXES, None, None, None)
    weights = P("section", None, None)
    return jax.shard_map(
        on_device,
        mesh=fine_mesh(mesh),
        in_specs=(
            tiles, tiles, weights, weights, weights, P("section", None), P("section", None), P(), P(),
        ),
        out_specs=(owned, owned, weights, weights, weights),
        check_vma=False,
    )
```

```python
import jax
import jax.numpy as jnp
from jax import lax
from jax.experimental import pallas as pl
from jax.experimental.pallas import tpu as pltpu
from jax.sharding import Mesh
from jax.sharding import PartitionSpec as P

TILE_AXES = ("z", "y", "core")
SIDE = 16
REGION = 32
HALO = 8
RIM = 4
PIXELS = REGION * REGION
WIDTH = 64
CHANS = 256
BF = jnp.bfloat16
F32 = jnp.float32
VMEM_LIMIT = 56 * 1024 * 1024


def mm(left, right):
    return jnp.dot(left, right, preferred_element_type=F32)


def mm_first(left, right):
    return lax.dot_general(left, right, (((0,), (0,)), ((), ())), preferred_element_type=F32)


def silu_parts(value):
    sig = 0.5 + 0.5 * jnp.tanh(0.5 * value)
    out = value * sig
    return (out, sig + out * (1.0 - sig))


def around(tile, owner, near):
    north, south = (near[tile * 4], near[tile * 4 + 1])
    west, east = (near[tile * 4 + 2], near[tile * 4 + 3])

    def step(first, way, second, other):
        one = jnp.where(first >= 0, near[jnp.maximum(first, 0) * 4 + way], -1)
        two = jnp.where(second >= 0, near[jnp.maximum(second, 0) * 4 + other], -1)
        return jnp.where(one >= 0, one, two)

    ids = [
        step(north, 2, west, 0), north, step(north, 3, east, 0),
        west, tile, east,
        step(south, 2, west, 1), south, step(south, 3, east, 1),
    ]
    found = [item >= 0 for item in ids]
    rows = [owner[jnp.maximum(item, 0)] for item in ids]
    return (rows, found)


def pool_place(row, here):
    device, slot = (row >> 2, row & 3)
    gap = (device >> 1) - (here >> 1)
    side = jnp.where(gap < 0, 0, 1)
    near = jnp.where(gap == 0, 0, 4 + 4 * side) + slot
    same = (device & 1) == (here & 1)
    far = 12 + jnp.where(same, 4 * side, 0) + slot
    place = jnp.where(jnp.abs(gap) <= 1, near, far) + jnp.where(same, 0, 20)
    return jnp.clip(place, 0, 39)


def bands_of(halo):
    return (
        (HALO - halo, halo, 0, SIDE - halo),
        (HALO, SIDE, 3, 0),
        (HALO + SIDE, halo, 6, 0),
    )


def build_region(pool, region, lane, places, found, halo):
    for top, rows, first, start in bands_of(halo):
        parts = []
        for k in range(3):
            part = pool[places[first + k], pl.ds(start, rows)].astype(F32)
            part = jnp.where(found[first + k], part, 0.0)
            cut = (slice(HALO, SIDE), slice(0, SIDE), slice(0, HALO))[k]
            parts.append(part[:, cut, :])
        band = jnp.concatenate(parts, axis=1).reshape(rows * REGION, CHANS).astype(BF)
        region[pl.ds(top * REGION, rows * REGION), pl.ds(lane * CHANS, CHANS)] = band


def build_present(present, found_pair):
    for top, rows, first, _ in bands_of(HALO):
        shape = (rows * REGION, 2 * WIDTH)
        col = lax.broadcasted_iota(jnp.int32, shape, 0) % REGION
        lane = lax.broadcasted_iota(jnp.int32, shape, 1)
        sides = []
        for found in found_pair:
            flags = [jnp.where(found[first + k], 1.0, 0.0) for k in range(3)]
            sides.append(
                jnp.where(col < HALO, flags[0], jnp.where(col < HALO + SIDE, flags[1], flags[2]))
            )
        present[pl.ds(top * REGION, rows * REGION), :] = jnp.where(lane < WIDTH, sides[0], sides[1])


def build_masks(masks):
    shape = (PIXELS, 2 * WIDTH)
    pixel = lax.broadcasted_iota(jnp.int32, shape, 0)
    row, col = (pixel // REGION, pixel % REGION)
    low, high = (HALO, HALO + SIDE)
    west = (col == low) | (col == high)
    east = (col == low - 1) | (col == high - 1)
    above = (row == low - 1) | (row == high - 1)
    below = (row == low) | (row == high)
    for k, (across, along) in enumerate(
        ((above, west), (above, east), (below, west), (below, east))
    ):
        masks[k] = jnp.where(across & along, 0.0, 1.0).astype(BF)


def low_lanes(rows):
    return lax.broadcasted_iota(jnp.int32, (rows, 2 * WIDTH), 1) < WIDTH


def build_gates(gates):
    col = lax.broadcasted_iota(jnp.int32, (4 * REGION, 2 * WIDTH), 0) % REGION
    west = (col == HALO) | (col == HALO + SIDE)
    east = (col == HALO - 1) | (col == HALO + SIDE - 1)
    left = jnp.where(west & low_lanes(4 * REGION), 0.0, 1.0).astype(BF)
    gates[:, 0:128] = left
    gates[:, 128:256] = left
    gates[:, 256:384] = jnp.where(east, 0.0, 1.0).astype(BF)


def store_shifted(stack, center, start, value):
    count = value.shape[0]
    rows = pl.ds(start, count)
    low = low_lanes(count)
    other = pltpu.roll(value, WIDTH, 1)
    left = pltpu.roll(value, 1, 0)
    other_left = pltpu.roll(other, 1, 0)
    right = pltpu.roll(value, count - 1, 0)
    stack[rows, 0:128] = jnp.where(low, left, other).astype(BF)
    stack[rows, 128:256] = jnp.where(low, other_left, value).astype(BF)
    stack[rows, 256:384] = right.astype(BF)
    center[rows, :] = value.astype(BF)


def row_products(first, second, third, weights):
    one = mm(jnp.concatenate([first, third], axis=1), weights[0])
    two = mm(jnp.concatenate([second, third], axis=1), weights[1])
    low = low_lanes(first.shape[0])
    above = jnp.where(low, one[:, :128], two[:, :128])
    level = pltpu.roll(jnp.where(low, two[:, :128], one[:, :128]), WIDTH, 1)
    return (above, level, one[:, 128:] + two[:, 128:])


def convolve(stack, gates, products, start, count, weights):
    rows = pl.ds(start, count)
    parts = row_products(stack[rows, 0:128], stack[rows, 128:256], stack[rows, 256:384], weights)
    for k in range(3):
        products[k, rows, :] = parts[k]
    upper, lower = ((HALO - 1) * REGION, (HALO + SIDE - 1) * REGION)
    pair = 2 * REGION
    edge = jnp.concatenate([stack[pl.ds(upper, pair), :], stack[pl.ds(lower, pair), :]])
    edge = edge * gates[...]
    above, _, below = row_products(edge[:, 0:128], edge[:, 128:256], edge[:, 256:384], weights)
    for k, at in enumerate((upper, lower)):
        products[0, pl.ds(at, REGION), :] = above[k * pair : k * pair + REGION]
        products[2, pl.ds(at + REGION, REGION), :] = below[k * pair + REGION : (k + 1) * pair]
    inner = pl.ds(start + REGION, count - pair)
    return (
        products[0, pl.ds(start, count - pair), :]
        + products[1, inner, :]
        + products[2, pl.ds(start + pair, count - pair), :]
    )


def pool_copies(sources, pools, stored, weights, sems):
    feats, cots = ([], [])

    def add(group, source, target):
        sem = sems.at[len(feats) + len(cots)]
        group.append(pltpu.make_async_copy(source, target, sem))

    for core in range(2):
        at = 20 * core
        for source in sources[core][:3]:
            add(feats, source.at[pl.ds(0, 4)], pools[0].at[pl.ds(at, 4)])
            add(cots, source.at[pl.ds(4, 4)], pools[1].at[pl.ds(at, 4)])
            at += 4
        for source in sources[core][3:]:
            for k in range(4):
                add(feats, source.at[pl.ds(k * SIDE, SIDE)], pools[0].at[at])
                for end in range(2):
                    add(
                        cots,
                        source.at[pl.ds(4 * (SIDE + end * RIM) + k * RIM, RIM)],
                        pools[1].at[at, pl.ds(end * (SIDE - RIM), RIM)],
                    )
                at += 1
    for k, (source, target) in enumerate(zip(stored, weights)):
        add(feats if k < 3 else cots, source, target)
    return (feats, cots)


COPIES = 2 * 3 * 2 + 12 * 3 + 6


def inner_tile(region, lane):
    value = region[pl.ds(HALO * REGION, SIDE * REGION), pl.ds(lane * CHANS, CHANS)].astype(F32)
    value = value.reshape(SIDE, REGION, CHANS)[:, HALO : HALO + SIDE, :]
    return value.astype(BF)


INNER = (HALO * REGION, SIDE * REGION)


def fold_pair(value, rows, cols):
    return value[:rows, :cols] + value[rows:, cols:]


def whole_kernel(meta, owner, near, *refs):
    sources, stored, refs = ((refs[:5], refs[5:9]), refs[9:15], refs[15:])
    weights, refs = (refs[-6:], refs[:-6])
    w_red, w_tap, w_exp, v_red, v_tap, v_exp = weights
    (norms, out, grad_in, grads,
     feats, cots, sems, region, present, masks, gates, stack, center, products, s_one, s_two, s_three,
     a_own, h_one, h_two, d_one, total) = refs
    pair = pl.program_id(0)
    here, section = (meta[0], meta[1])
    copies = pool_copies(sources, (feats, cots), stored, weights, sems)

    @pl.when(pair == 0)
    def _():
        for group in copies:
            for copy in group:
                copy.start()
        build_masks(masks)
        build_gates(gates)
        total[...] = jnp.zeros_like(total)
        for copy in copies[0]:
            copy.wait()

    founds, places = ([], [])
    for lane in range(2):
        rows, found = around(meta[2 + pair * 2 + lane], owner, near)
        place = [pool_place(row, here) for row in rows]
        build_region(feats, region, lane, place, found, HALO)
        founds.append(found)
        places.append(place)
    build_present(present, founds)

    def ahead(b, carry):
        mine = b == section

        @pl.when(mine)
        def _():
            a_own[...] = region[pl.ds(*INNER), :]

        def front():
            start, count = (0, PIXELS)
            rows = pl.ds(start, count)
            pre = mm(region[rows, :], w_red[b]) * norms[b, 0:1, :128] + norms[b, 1:2, :128]
            hidden, slope = silu_parts(pre)
            there = present[rows, :]
            s_one[b, rows, :] = (slope * there * norms[b, 0:1, :128]).astype(BF)
            store_shifted(stack, center, start, hidden * there)

        front()

        def tail():
            start, count = (REGION, PIXELS - 2 * REGION)
            rows = pl.ds(start, count)
            pre = convolve(stack, gates, products, 0, PIXELS, w_tap[b])
            pre = pre * norms[b, 2:3, :128] + norms[b, 3:4, :128]
            hidden, slope = silu_parts(pre)
            s_two[b, rows, :] = (slope * norms[b, 2:3, :128]).astype(BF)
            hidden = hidden.astype(BF)

            @pl.when(mine)
            def _():
                h_two[rows, :] = hidden

            pre = (
                region[rows, :].astype(F32)
                + mm(hidden, w_exp[b]) * norms[b, 4:5, :]
                + norms[b, 5:6, :]
            )
            value, slope = silu_parts(pre)
            region[rows, :] = value.astype(BF)
            s_three[b, rows, :] = slope.astype(BF)

        tail()

        @pl.when(mine)
        def _():
            h_one[...] = center[...]
            out[0] = inner_tile(region, 0)
            out[1] = inner_tile(region, 1)

        return carry

    lax.fori_loop(0, 4, ahead, 0)

    @pl.when(pair == 0)
    def _():
        for copy in copies[1]:
            copy.wait()

    for lane in range(2):
        build_region(cots, region, lane, places[lane], founds[lane], RIM)

    def keep_inner(value):
        col = lax.broadcasted_iota(jnp.int32, value.shape, 0) % REGION
        return jnp.where((col >= HALO) & (col < HALO + SIDE), value, 0.0).astype(BF)

    def back(step, carry):
        b = 3 - step
        mine = b == section

        def first():
            start, count = (4 * REGION, PIXELS - 8 * REGION)
            rows = pl.ds(start, count)
            d_three = region[rows, :].astype(F32) * s_three[b, rows, :].astype(F32)
            e_three = (d_three * norms[b, 4:5, :]).astype(BF)
            d_two = mm(e_three, v_exp[b]) * s_two[b, rows, :].astype(F32)
            store_shifted(stack, center, start, d_two)

        first()

        @pl.when(mine)
        def _():
            rows = pl.ds(*INNER)
            d_three = region[rows, :].astype(F32) * s_three[b, rows, :].astype(F32)
            e_three = keep_inner(d_three * norms[b, 4:5, :])
            total_e = fold_pair(mm_first(h_two[rows, :], e_three), WIDTH, CHANS)
            total[416:480, :] += total_e[:, :128]
            total[480:544, :] += total_e[:, 128:]
            d_two = keep_inner(center[rows, :].astype(F32))
            around_rows = pl.ds(INNER[0] - REGION, INNER[1] + 2 * REGION)
            hidden = h_one[around_rows, :].astype(F32)
            left = pltpu.roll(hidden, 1, 0).astype(BF)
            right = pltpu.roll(hidden, hidden.shape[0] - 1, 0).astype(BF)
            middle = hidden.astype(BF)
            gated = [
                (left * masks[0, around_rows, :], 0), (middle, 0), (right * masks[1, around_rows, :], 0),
                (left, 1), (middle, 1), (right, 1),
                (left * masks[2, around_rows, :], 2), (middle, 2), (right * masks[3, around_rows, :], 2),
            ]
            for tap, (value, dy) in enumerate(gated):
                column = value[dy * REGION : dy * REGION + INNER[1]]
                piece = fold_pair(mm_first(column, d_two), WIDTH, WIDTH)
                if tap < 4:
                    total[tap * 64 : tap * 64 + 64, :64] += piece
                elif tap > 4:
                    at = (tap - 5) * 64 + 32
                    total[at : at + 64, 64:] += piece
                else:
                    total[256:288, :64] += piece[:32]
                    total[0:32, 64:] += piece[32:]

        def second():
            start, count = (5 * REGION, PIXELS - 10 * REGION)
            rows = pl.ds(start, count)
            d_hidden = convolve(
                stack, gates, products, 4 * REGION, PIXELS - 8 * REGION, v_tap[b]
            )
            d_first = (d_hidden * s_one[b, rows, :].astype(F32)).astype(BF)
            d_one[rows, :] = d_first
            d_three = region[rows, :].astype(F32) * s_three[b, rows, :].astype(F32)
            region[rows, :] = (d_three + mm(d_first, v_red[b])).astype(BF)

        second()

        @pl.when(mine)
        def _():
            rows = pl.ds(*INNER)
            d_first = keep_inner(d_one[rows, :].astype(F32))
            piece = fold_pair(mm_first(a_own[...], d_first), CHANS, WIDTH)
            total[288:416, :64] += piece[:128]
            total[288:416, 64:] += piece[128:]
            grad_in[0] = inner_tile(region, 0)
            grad_in[1] = inner_tile(region, 1)

        return carry

    lax.fori_loop(0, 4, back, 0)

    @pl.when(pair == 1)
    def _():
        grads[...] = total[...].astype(BF)


def run_kernel(scalars, sources, weights):
    def whole(item):
        return pl.BlockSpec(item.shape, lambda i, *_, n=len(item.shape): (0,) * n)

    tiles = jax.ShapeDtypeStruct((4, SIDE, SIDE, CHANS), BF)
    grads = jax.ShapeDtypeStruct((640, 128), BF)
    pair = pl.BlockSpec((2, SIDE, SIDE, CHANS), lambda i, *_: (i, 0, 0, 0))
    narrow = (PIXELS, 2 * WIDTH)
    pool = pltpu.VMEM((40, SIDE, SIDE, CHANS), BF)
    wide = (PIXELS, 2 * CHANS)
    return pl.pallas_call(
        whole_kernel,
        grid_spec=pltpu.PrefetchScalarGridSpec(
            num_scalar_prefetch=len(scalars),
            grid=(2,),
            in_specs=[pl.BlockSpec(memory_space=pl.ANY)] * (len(sources) + 6)
            + [whole(weights[6])],
            out_specs=[pair, pair, whole(grads)],
            scratch_shapes=[
                pool,
                pool,
                pltpu.SemaphoreType.DMA((COPIES,)),
                pltpu.VMEM(wide, BF),
                pltpu.VMEM(narrow, F32),
                pltpu.VMEM((4,) + narrow, BF),
                pltpu.VMEM((4 * REGION, 6 * WIDTH), BF),
                pltpu.VMEM((PIXELS, 6 * WIDTH), BF),
                pltpu.VMEM(narrow, BF),
                pltpu.VMEM((3,) + narrow, F32),
                pltpu.VMEM((4,) + narrow, BF),
                pltpu.VMEM((4,) + narrow, BF),
                pltpu.VMEM((4,) + wide, BF),
                pltpu.VMEM((INNER[1], 2 * CHANS), BF),
                pltpu.VMEM(narrow, BF),
                pltpu.VMEM(narrow, BF),
                pltpu.VMEM(narrow, BF),
                pltpu.VMEM((640, 128), F32),
                *[pltpu.VMEM(item.shape, BF) for item in weights[:6]],
            ],
        ),
        out_shape=[tiles, tiles, grads],
        compiler_params=pltpu.CompilerParams(
            dimension_semantics=("arbitrary",), vmem_limit_bytes=VMEM_LIMIT
        ),
    )(*scalars, *sources, *weights)


def shift(block, axes, distance):
    devices = range(lax.axis_size(axes))
    return lax.ppermute(block, axes, [(i, i + distance) for i in devices if i + distance in devices])


def other_core(block):
    return lax.ppermute(block, "core", [(0, 1), (1, 0)])


def trimmed(both):
    ends = (both[4:, :RIM], both[4:, SIDE - RIM :])
    return jnp.concatenate([item.reshape(-1, SIDE, CHANS) for item in (both[:4], *ends)])


def reach_close(features, cotangent):
    both = jnp.concatenate([features, cotangent])
    return [both, shift(both, TILE_AXES, 2), shift(both, TILE_AXES, -2)]


def reach_far(column):
    return [
        shift(trimmed(column[1]), TILE_AXES, 2),
        shift(trimmed(column[2]), TILE_AXES, -2),
    ]


def swap_cores(column, far, early):
    needed = jnp.where(lax.axis_index("core") == 0, far[1], far[0])
    swapped = [other_core(column[0]), early, other_core(column[2]), other_core(needed)]
    return [*column, *far, *swapped]


def swap_chunks(parts, axes):
    return lax.all_to_all(parts, axes, 0, 0, tiled=True)


def sum_over_tiles(values):
    plane = ("y", "core")
    across = lax.axis_size(plane)
    rows = values.shape[0] // across
    got = swap_chunks(values, plane).reshape(across, rows, 128)
    mine = jnp.sum(got.astype(F32), axis=0).astype(BF)
    got = swap_chunks(jnp.tile(mine, (lax.axis_size("z"), 1)), "z").reshape(-1, rows, 128)
    total = jnp.sum(got.astype(F32), axis=0).astype(BF)
    return swap_chunks(jnp.tile(total, (across, 1)), plane).astype(F32)


def split_float(value):
    high = value.astype(BF)
    low = (value - high.astype(F32)).astype(BF)
    return (high, low)


def gather_params(pieces):
    packed = jnp.concatenate([item.reshape(-1, 128) for item in pieces])
    return lax.all_gather(packed, "section", axis=0, tiled=False)


def cut_params(every, pieces):
    at = 0
    cut = []
    for item in pieces:
        rows = item.size // 128
        cut.append(every[:, at : at + rows].reshape((-1,) + item.shape[1:]))
        at += rows
    scale = cut[3].astype(F32) + cut[4].astype(F32)
    offset = cut[5].astype(F32) + cut[6].astype(F32)
    return (cut[0], cut[1], cut[2], scale, offset)


def twice(weights):
    zero = jnp.zeros_like(weights)
    return jnp.concatenate(
        [jnp.concatenate([weights, zero], axis=-1), jnp.concatenate([zero, weights], axis=-1)],
        axis=-2,
    )


def tap_pair(taps):
    blank = jnp.zeros_like(taps[:, 0, 0])

    def grid(rows, cols):
        lines = []
        for dx in rows:
            line = [blank if None in (dx, dy) else taps[:, dy, dx] for dy in cols]
            lines.append(jnp.concatenate(line, axis=2))
        return jnp.concatenate(lines, axis=1)

    return jnp.stack([grid((0, 1, 2, None), (0, 1, 2, None)), grid((0, 1, None, 2), (1, 0, None, 2))], axis=1)


def norm_rows(scale, offset):
    rows = []
    for low, high in ((0, 64), (64, 128), (128, 384)):
        for item in (scale, offset):
            part = jnp.concatenate([item[:, low:high]] * 2, axis=1)
            rows.append(jnp.pad(part, ((0, 0), (0, 512 - part.shape[1]))))
    rows.extend([jnp.zeros_like(rows[0])] * 2)
    return jnp.stack(rows, axis=1)


def on_device(
    features, out_cotangent, w_reduce, w_taps, w_expand, norm_scale, norm_shift, owner, neighbours
):
    here = lax.axis_index(TILE_AXES).astype(jnp.int32)
    section = lax.axis_index("section").astype(jnp.int32)
    slots = here * 4 + jnp.arange(4, dtype=jnp.int32)
    hit = owner[None, :] == slots[:, None]
    ids = jnp.sum(
        jnp.where(hit, jnp.arange(owner.shape[0], dtype=jnp.int32)[None, :], 0), axis=1
    )
    meta = jnp.concatenate([here[None], section[None], ids.astype(jnp.int32)])
    scalars = (meta, owner, neighbours.reshape(-1))

    pieces = [w_reduce, w_taps, w_expand, *split_float(norm_scale), *split_float(norm_shift)]
    column = reach_close(features, out_cotangent)
    column, every = lax.optimization_barrier((column, gather_params(pieces)))
    far = reach_far(column)
    early = other_core(column[1])
    every, early = lax.optimization_barrier((every, early))
    w_red, w_tap, w_exp, scale, offset = cut_params(every, pieces)
    taps = w_tap.reshape(4, 3, 3, WIDTH, WIDTH)
    turned = taps[:, ::-1, ::-1].swapaxes(3, 4)
    weights = (
        twice(w_red),
        tap_pair(taps),
        twice(w_exp),
        twice(w_red.swapaxes(1, 2)),
        tap_pair(turned),
        twice(w_exp.swapaxes(1, 2)),
        norm_rows(scale, offset),
    )
    far, weights = lax.optimization_barrier((far, weights))
    sources = swap_cores(column, far, early)
    out, grad_in, grads = run_kernel(scalars, sources, weights)
    total = sum_over_tiles(grads)
    g_taps = jnp.concatenate([total[:288, :64], total[:288, 64:]])
    g_reduce = jnp.concatenate([total[288:416, :64], total[288:416, 64:]])
    g_expand = jnp.concatenate([total[416:480], total[480:544]], axis=1)
    return (out[None], grad_in[None], g_reduce[None], g_taps[None], g_expand[None])


def fine_mesh(mesh):
    shape = (mesh.devices.shape[0], mesh.devices.shape[1] // 16, 8, 2)
    return Mesh(mesh.devices.reshape(shape), ("section",) + TILE_AXES)


def solution(mesh):
    tiles = P(TILE_AXES, None, None, None)
    owned = P("section", TILE_AXES, None, None, None)
    weights = P("section", None, None)
    return jax.shard_map(
        on_device,
        mesh=fine_mesh(mesh),
        in_specs=(
            tiles, tiles, weights, weights, weights, P("section", None), P("section", None), P(), P(),
        ),
        out_specs=(owned, owned, weights, weights, weights),
        check_vma=False,
    )
```

```python
import jax
import jax.numpy as jnp
from jax import lax
from jax.experimental import pallas as pl
from jax.experimental.pallas import tpu as pltpu
from jax.sharding import Mesh
from jax.sharding import PartitionSpec as P

TILE_AXES = ("z", "y", "core")
SIDE = 16
REGION = 32
HALO = 8
RIM = 4
PIXELS = REGION * REGION
WIDTH = 64
CHANS = 256
BF = jnp.bfloat16
F32 = jnp.float32
VMEM_LIMIT = 56 * 1024 * 1024


def mm(left, right):
    return jnp.dot(left, right, preferred_element_type=F32)


def mm_first(left, right):
    return lax.dot_general(left, right, (((0,), (0,)), ((), ())), preferred_element_type=F32)


def silu_parts(value):
    sig = 0.5 + 0.5 * jnp.tanh(0.5 * value)
    out = value * sig
    return (out, sig + out * (1.0 - sig))


def around(tile, owner, near):
    north, south = (near[tile * 4], near[tile * 4 + 1])
    west, east = (near[tile * 4 + 2], near[tile * 4 + 3])

    def step(first, way, second, other):
        one = jnp.where(first >= 0, near[jnp.maximum(first, 0) * 4 + way], -1)
        two = jnp.where(second >= 0, near[jnp.maximum(second, 0) * 4 + other], -1)
        return jnp.where(one >= 0, one, two)

    ids = [
        step(north, 2, west, 0), north, step(north, 3, east, 0),
        west, tile, east,
        step(south, 2, west, 1), south, step(south, 3, east, 1),
    ]
    found = [item >= 0 for item in ids]
    rows = [owner[jnp.maximum(item, 0)] for item in ids]
    return (rows, found)


def pool_place(row, here):
    device, slot = (row >> 2, row & 3)
    gap = (device >> 1) - (here >> 1)
    side = jnp.where(gap < 0, 0, 1)
    near = jnp.where(gap == 0, 0, 4 + 4 * side) + slot
    same = (device & 1) == (here & 1)
    far = 12 + jnp.where(same, 4 * side, 0) + slot
    place = jnp.where(jnp.abs(gap) <= 1, near, far) + jnp.where(same, 0, 20)
    return jnp.clip(place, 0, 39)


def bands_of(halo):
    return (
        (HALO - halo, halo, 0, SIDE - halo),
        (HALO, SIDE, 3, 0),
        (HALO + SIDE, halo, 6, 0),
    )


def build_region(pool, region, lane, places, found, halo):
    for top, rows, first, start in bands_of(halo):
        parts = []
        for k in range(3):
            part = pool[places[first + k], pl.ds(start, rows)].astype(F32)
            part = jnp.where(found[first + k], part, 0.0)
            cut = (slice(HALO, SIDE), slice(0, SIDE), slice(0, HALO))[k]
            parts.append(part[:, cut, :])
        band = jnp.concatenate(parts, axis=1).reshape(rows * REGION, CHANS).astype(BF)
        region[pl.ds(top * REGION, rows * REGION), pl.ds(lane * CHANS, CHANS)] = band


def build_present(present, found_pair):
    for top, rows, first, _ in bands_of(HALO):
        shape = (rows * REGION, 2 * WIDTH)
        col = lax.broadcasted_iota(jnp.int32, shape, 0) % REGION
        lane = lax.broadcasted_iota(jnp.int32, shape, 1)
        sides = []
        for found in found_pair:
            flags = [jnp.where(found[first + k], 1.0, 0.0) for k in range(3)]
            sides.append(
                jnp.where(col < HALO, flags[0], jnp.where(col < HALO + SIDE, flags[1], flags[2]))
            )
        present[pl.ds(top * REGION, rows * REGION), :] = jnp.where(lane < WIDTH, sides[0], sides[1])


def build_masks(masks):
    shape = (PIXELS, 2 * WIDTH)
    pixel = lax.broadcasted_iota(jnp.int32, shape, 0)
    row, col = (pixel // REGION, pixel % REGION)
    low, high = (HALO, HALO + SIDE)
    west = (col == low) | (col == high)
    east = (col == low - 1) | (col == high - 1)
    above = (row == low - 1) | (row == high - 1)
    below = (row == low) | (row == high)
    for k, (across, along) in enumerate(
        ((above, west), (above, east), (below, west), (below, east))
    ):
        masks[k] = jnp.where(across & along, 0.0, 1.0).astype(BF)


def low_lanes(rows):
    return lax.broadcasted_iota(jnp.int32, (rows, 2 * WIDTH), 1) < WIDTH


def build_gates(gates):
    col = lax.broadcasted_iota(jnp.int32, (4 * REGION, 2 * WIDTH), 0) % REGION
    west = (col == HALO) | (col == HALO + SIDE)
    east = (col == HALO - 1) | (col == HALO + SIDE - 1)
    left = jnp.where(west & low_lanes(4 * REGION), 0.0, 1.0).astype(BF)
    gates[:, 0:128] = left
    gates[:, 128:256] = left
    gates[:, 256:384] = jnp.where(east, 0.0, 1.0).astype(BF)


def store_shifted(stack, center, start, value):
    count = value.shape[0]
    rows = pl.ds(start, count)
    low = low_lanes(count)
    other = pltpu.roll(value, WIDTH, 1)
    left = pltpu.roll(value, 1, 0)
    other_left = pltpu.roll(other, 1, 0)
    right = pltpu.roll(value, count - 1, 0)
    stack[rows, 0:128] = jnp.where(low, left, other).astype(BF)
    stack[rows, 128:256] = jnp.where(low, other_left, value).astype(BF)
    stack[rows, 256:384] = right.astype(BF)
    center[rows, :] = value.astype(BF)


def row_products(first, second, third, weights):
    one = mm(jnp.concatenate([first, third], axis=1), weights[0])
    two = mm(jnp.concatenate([second, third], axis=1), weights[1])
    low = low_lanes(first.shape[0])
    above = jnp.where(low, one[:, :128], two[:, :128])
    level = pltpu.roll(jnp.where(low, two[:, :128], one[:, :128]), WIDTH, 1)
    return (above, level, one[:, 128:] + two[:, 128:])


def convolve(stack, gates, products, start, count, weights):
    rows = pl.ds(start, count)
    parts = row_products(stack[rows, 0:128], stack[rows, 128:256], stack[rows, 256:384], weights)
    for k in range(3):
        products[k, rows, :] = parts[k]
    upper, lower = ((HALO - 1) * REGION, (HALO + SIDE - 1) * REGION)
    pair = 2 * REGION
    edge = jnp.concatenate([stack[pl.ds(upper, pair), :], stack[pl.ds(lower, pair), :]])
    edge = edge * gates[...]
    above, _, below = row_products(edge[:, 0:128], edge[:, 128:256], edge[:, 256:384], weights)
    for k, at in enumerate((upper, lower)):
        products[0, pl.ds(at, REGION), :] = above[k * pair : k * pair + REGION]
        products[2, pl.ds(at + REGION, REGION), :] = below[k * pair + REGION : (k + 1) * pair]
    inner = pl.ds(start + REGION, count - pair)
    return (
        products[0, pl.ds(start, count - pair), :]
        + products[1, inner, :]
        + products[2, pl.ds(start + pair, count - pair), :]
    )


def pool_copies(sources, pools, stored, weights, sems):
    feats, cots = ([], [])

    def add(group, source, target):
        sem = sems.at[len(feats) + len(cots)]
        group.append(pltpu.make_async_copy(source, target, sem))

    for core in range(2):
        at = 20 * core
        for source in sources[core][:3]:
            add(feats, source.at[pl.ds(0, 4)], pools[0].at[pl.ds(at, 4)])
            add(cots, source.at[pl.ds(4, 4)], pools[1].at[pl.ds(at, 4)])
            at += 4
        for source in sources[core][3:]:
            for k in range(4):
                add(feats, source.at[pl.ds(k * SIDE, SIDE)], pools[0].at[at])
                for end in range(2):
                    add(
                        cots,
                        source.at[pl.ds(4 * (SIDE + end * RIM) + k * RIM, RIM)],
                        pools[1].at[at, pl.ds(end * (SIDE - RIM), RIM)],
                    )
                at += 1
    for k, (source, target) in enumerate(zip(stored, weights)):
        add(feats if k < 3 else cots, source, target)
    return (feats, cots)


COPIES = 2 * 3 * 2 + 12 * 3 + 6


def inner_tile(region, lane):
    value = region[pl.ds(HALO * REGION, SIDE * REGION), pl.ds(lane * CHANS, CHANS)].astype(F32)
    value = value.reshape(SIDE, REGION, CHANS)[:, HALO : HALO + SIDE, :]
    return value.astype(BF)


INNER = (HALO * REGION, SIDE * REGION)


def fold_pair(value, rows, cols):
    return value[:rows, :cols] + value[rows:, cols:]


def whole_kernel(meta, owner, near, *refs):
    sources, stored, refs = ((refs[:5], refs[5:9]), refs[9:15], refs[15:])
    weights, refs = (refs[-6:], refs[:-6])
    w_red, w_tap, w_exp, v_red, v_tap, v_exp = weights
    (norms, out, grad_in, grads,
     feats, cots, sems, region, present, masks, gates, stack, center, products, s_one, s_two, s_three,
     a_own, h_one, h_two, d_one, total) = refs
    pair = pl.program_id(0)
    here, section = (meta[0], meta[1])
    copies = pool_copies(sources, (feats, cots), stored, weights, sems)

    @pl.when(pair == 0)
    def _():
        for group in copies:
            for copy in group:
                copy.start()
        build_masks(masks)
        build_gates(gates)
        total[...] = jnp.zeros_like(total)
        for copy in copies[0]:
            copy.wait()

    founds, places = ([], [])
    for lane in range(2):
        rows, found = around(meta[2 + pair * 2 + lane], owner, near)
        place = [pool_place(row, here) for row in rows]
        build_region(feats, region, lane, place, found, HALO)
        founds.append(found)
        places.append(place)
    build_present(present, founds)

    def ahead(b, carry):
        mine = b == section

        @pl.when(mine)
        def _():
            a_own[...] = region[pl.ds(*INNER), :]

        def front():
            start, count = (0, PIXELS)
            rows = pl.ds(start, count)
            pre = mm(region[rows, :], w_red[b]) * norms[b, 0:1, :128] + norms[b, 1:2, :128]
            hidden, slope = silu_parts(pre)
            there = present[rows, :]
            s_one[b, rows, :] = (slope * there * norms[b, 0:1, :128]).astype(BF)
            store_shifted(stack, center, start, hidden * there)

        front()

        def tail():
            start, count = (REGION, PIXELS - 2 * REGION)
            rows = pl.ds(start, count)
            pre = convolve(stack, gates, products, 0, PIXELS, w_tap[b])
            pre = pre * norms[b, 2:3, :128] + norms[b, 3:4, :128]
            hidden, slope = silu_parts(pre)
            s_two[b, rows, :] = (slope * norms[b, 2:3, :128]).astype(BF)
            hidden = hidden.astype(BF)

            @pl.when(mine)
            def _():
                h_two[rows, :] = hidden

            pre = (
                region[rows, :].astype(F32)
                + mm(hidden, w_exp[b]) * norms[b, 4:5, :]
                + norms[b, 5:6, :]
            )
            value, slope = silu_parts(pre)
            region[rows, :] = value.astype(BF)
            s_three[b, rows, :] = slope.astype(BF)

        tail()

        @pl.when(mine)
        def _():
            h_one[...] = center[...]
            out[0] = inner_tile(region, 0)
            out[1] = inner_tile(region, 1)

        return carry

    lax.fori_loop(0, 4, ahead, 0)

    @pl.when(pair == 0)
    def _():
        for copy in copies[1]:
            copy.wait()

    for lane in range(2):
        build_region(cots, region, lane, places[lane], founds[lane], RIM)

    def keep_inner(value):
        col = lax.broadcasted_iota(jnp.int32, value.shape, 0) % REGION
        return jnp.where((col >= HALO) & (col < HALO + SIDE), value, 0.0).astype(BF)

    def back(step, carry):
        b = 3 - step
        mine = b == section

        def first():
            start, count = (4 * REGION, PIXELS - 8 * REGION)
            rows = pl.ds(start, count)
            d_three = region[rows, :].astype(F32) * s_three[b, rows, :].astype(F32)
            e_three = (d_three * norms[b, 4:5, :]).astype(BF)
            d_two = mm(e_three, v_exp[b]) * s_two[b, rows, :].astype(F32)
            store_shifted(stack, center, start, d_two)

        first()

        @pl.when(mine)
        def _():
            rows = pl.ds(*INNER)
            d_three = region[rows, :].astype(F32) * s_three[b, rows, :].astype(F32)
            e_three = keep_inner(d_three * norms[b, 4:5, :])
            total_e = fold_pair(mm_first(h_two[rows, :], e_three), WIDTH, CHANS)
            total[416:480, :] += total_e[:, :128]
            total[480:544, :] += total_e[:, 128:]
            d_two = keep_inner(center[rows, :].astype(F32))
            around_rows = pl.ds(INNER[0] - REGION, INNER[1] + 2 * REGION)
            hidden = h_one[around_rows, :].astype(F32)
            left = pltpu.roll(hidden, 1, 0).astype(BF)
            right = pltpu.roll(hidden, hidden.shape[0] - 1, 0).astype(BF)
            middle = hidden.astype(BF)
            gated = [
                (left * masks[0, around_rows, :], 0), (middle, 0), (right * masks[1, around_rows, :], 0),
                (left, 1), (middle, 1), (right, 1),
                (left * masks[2, around_rows, :], 2), (middle, 2), (right * masks[3, around_rows, :], 2),
            ]
            for tap, (value, dy) in enumerate(gated):
                column = value[dy * REGION : dy * REGION + INNER[1]]
                piece = fold_pair(mm_first(column, d_two), WIDTH, WIDTH)
                if tap < 4:
                    total[tap * 64 : tap * 64 + 64, :64] += piece
                elif tap > 4:
                    at = (tap - 5) * 64 + 32
                    total[at : at + 64, 64:] += piece
                else:
                    total[256:288, :64] += piece[:32]
                    total[0:32, 64:] += piece[32:]

        def second():
            start, count = (5 * REGION, PIXELS - 10 * REGION)
            rows = pl.ds(start, count)
            d_hidden = convolve(
                stack, gates, products, 4 * REGION, PIXELS - 8 * REGION, v_tap[b]
            )
            d_first = (d_hidden * s_one[b, rows, :].astype(F32)).astype(BF)
            d_one[rows, :] = d_first
            d_three = region[rows, :].astype(F32) * s_three[b, rows, :].astype(F32)
            region[rows, :] = (d_three + mm(d_first, v_red[b])).astype(BF)

        second()

        @pl.when(mine)
        def _():
            rows = pl.ds(*INNER)
            d_first = keep_inner(d_one[rows, :].astype(F32))
            piece = fold_pair(mm_first(a_own[...], d_first), CHANS, WIDTH)
            total[288:416, :64] += piece[:128]
            total[288:416, 64:] += piece[128:]
            grad_in[0] = inner_tile(region, 0)
            grad_in[1] = inner_tile(region, 1)

        return carry

    lax.fori_loop(0, 4, back, 0)

    @pl.when(pair == 1)
    def _():
        grads[...] = total[...].astype(BF)


def run_kernel(scalars, sources, weights):
    def whole(item):
        return pl.BlockSpec(item.shape, lambda i, *_, n=len(item.shape): (0,) * n)

    tiles = jax.ShapeDtypeStruct((4, SIDE, SIDE, CHANS), BF)
    grads = jax.ShapeDtypeStruct((640, 128), BF)
    pair = pl.BlockSpec((2, SIDE, SIDE, CHANS), lambda i, *_: (i, 0, 0, 0))
    narrow = (PIXELS, 2 * WIDTH)
    pool = pltpu.VMEM((40, SIDE, SIDE, CHANS), BF)
    wide = (PIXELS, 2 * CHANS)
    return pl.pallas_call(
        whole_kernel,
        grid_spec=pltpu.PrefetchScalarGridSpec(
            num_scalar_prefetch=len(scalars),
            grid=(2,),
            in_specs=[pl.BlockSpec(memory_space=pl.ANY)] * (len(sources) + 6)
            + [whole(weights[6])],
            out_specs=[pair, pair, whole(grads)],
            scratch_shapes=[
                pool,
                pool,
                pltpu.SemaphoreType.DMA((COPIES,)),
                pltpu.VMEM(wide, BF),
                pltpu.VMEM(narrow, F32),
                pltpu.VMEM((4,) + narrow, BF),
                pltpu.VMEM((4 * REGION, 6 * WIDTH), BF),
                pltpu.VMEM((PIXELS, 6 * WIDTH), BF),
                pltpu.VMEM(narrow, BF),
                pltpu.VMEM((3,) + narrow, F32),
                pltpu.VMEM((4,) + narrow, BF),
                pltpu.VMEM((4,) + narrow, BF),
                pltpu.VMEM((4,) + wide, BF),
                pltpu.VMEM((INNER[1], 2 * CHANS), BF),
                pltpu.VMEM(narrow, BF),
                pltpu.VMEM(narrow, BF),
                pltpu.VMEM(narrow, BF),
                pltpu.VMEM((640, 128), F32),
                *[pltpu.VMEM(item.shape, BF) for item in weights[:6]],
            ],
        ),
        out_shape=[tiles, tiles, grads],
        compiler_params=pltpu.CompilerParams(
            dimension_semantics=("arbitrary",), vmem_limit_bytes=VMEM_LIMIT
        ),
    )(*scalars, *sources, *weights)


def shift(block, axes, distance):
    devices = range(lax.axis_size(axes))
    return lax.ppermute(block, axes, [(i, i + distance) for i in devices if i + distance in devices])


def other_core(block):
    return lax.ppermute(block, "core", [(0, 1), (1, 0)])


def trimmed(both):
    ends = (both[4:, :RIM], both[4:, SIDE - RIM :])
    return jnp.concatenate([item.reshape(-1, SIDE, CHANS) for item in (both[:4], *ends)])


def reach_close(features, cotangent):
    both = jnp.concatenate([features, cotangent])
    return [both, shift(both, TILE_AXES, 2), shift(both, TILE_AXES, -2)]


def reach_far(sent):
    return [shift(sent[0], TILE_AXES, 2), shift(sent[1], TILE_AXES, -2)]


def swap_cores(column, far, early):
    needed = jnp.where(lax.axis_index("core") == 0, far[1], far[0])
    swapped = [other_core(column[0]), early, other_core(column[2]), other_core(needed)]
    return [*column, *far, *swapped]


def swap_chunks(parts, axes):
    return lax.all_to_all(parts, axes, 0, 0, tiled=True)


def sum_over_tiles(values):
    plane = ("y", "core")
    across = lax.axis_size(plane)
    rows = values.shape[0] // across
    got = swap_chunks(values, plane).reshape(across, rows, 128)
    mine = jnp.sum(got.astype(F32), axis=0).astype(BF)
    got = swap_chunks(jnp.tile(mine, (lax.axis_size("z"), 1)), "z").reshape(-1, rows, 128)
    total = jnp.sum(got.astype(F32), axis=0).astype(BF)
    return swap_chunks(jnp.tile(total, (across, 1)), plane).astype(F32)


def split_float(value):
    high = value.astype(BF)
    low = (value - high.astype(F32)).astype(BF)
    return (high, low)


def gather_params(pieces):
    packed = jnp.concatenate([item.reshape(-1, 128) for item in pieces])
    return lax.all_gather(packed, "section", axis=0, tiled=False)


def cut_params(every, pieces):
    at = 0
    cut = []
    for item in pieces:
        rows = item.size // 128
        cut.append(every[:, at : at + rows].reshape((-1,) + item.shape[1:]))
        at += rows
    scale = cut[3].astype(F32) + cut[4].astype(F32)
    offset = cut[5].astype(F32) + cut[6].astype(F32)
    return (cut[0], cut[1], cut[2], scale, offset)


def twice(weights):
    zero = jnp.zeros_like(weights)
    return jnp.concatenate(
        [jnp.concatenate([weights, zero], axis=-1), jnp.concatenate([zero, weights], axis=-1)],
        axis=-2,
    )


def tap_pair(taps):
    blank = jnp.zeros_like(taps[:, 0, 0])

    def grid(rows, cols):
        lines = []
        for dx in rows:
            line = [blank if None in (dx, dy) else taps[:, dy, dx] for dy in cols]
            lines.append(jnp.concatenate(line, axis=2))
        return jnp.concatenate(lines, axis=1)

    return jnp.stack([grid((0, 1, 2, None), (0, 1, 2, None)), grid((0, 1, None, 2), (1, 0, None, 2))], axis=1)


def norm_rows(scale, offset):
    rows = []
    for low, high in ((0, 64), (64, 128), (128, 384)):
        for item in (scale, offset):
            part = jnp.concatenate([item[:, low:high]] * 2, axis=1)
            rows.append(jnp.pad(part, ((0, 0), (0, 512 - part.shape[1]))))
    rows.extend([jnp.zeros_like(rows[0])] * 2)
    return jnp.stack(rows, axis=1)


def on_device(
    features, out_cotangent, w_reduce, w_taps, w_expand, norm_scale, norm_shift, owner, neighbours
):
    here = lax.axis_index(TILE_AXES).astype(jnp.int32)
    section = lax.axis_index("section").astype(jnp.int32)
    slots = here * 4 + jnp.arange(4, dtype=jnp.int32)
    hit = owner[None, :] == slots[:, None]
    ids = jnp.sum(
        jnp.where(hit, jnp.arange(owner.shape[0], dtype=jnp.int32)[None, :], 0), axis=1
    )
    meta = jnp.concatenate([here[None], section[None], ids.astype(jnp.int32)])
    scalars = (meta, owner, neighbours.reshape(-1))

    pieces = [w_reduce, w_taps, w_expand, *split_float(norm_scale), *split_float(norm_shift)]
    column = reach_close(features, out_cotangent)
    column, every = lax.optimization_barrier((column, gather_params(pieces)))
    sent = [trimmed(column[1]), trimmed(column[2])]
    column, sent = lax.optimization_barrier((column, sent))
    far = reach_far(sent)
    early = other_core(column[1])
    every, early = lax.optimization_barrier((every, early))
    w_red, w_tap, w_exp, scale, offset = cut_params(every, pieces)
    taps = w_tap.reshape(4, 3, 3, WIDTH, WIDTH)
    turned = taps[:, ::-1, ::-1].swapaxes(3, 4)
    weights = (
        twice(w_red),
        tap_pair(taps),
        twice(w_exp),
        twice(w_red.swapaxes(1, 2)),
        tap_pair(turned),
        twice(w_exp.swapaxes(1, 2)),
        norm_rows(scale, offset),
    )
    far, weights = lax.optimization_barrier((far, weights))
    sources = swap_cores(column, far, early)
    out, grad_in, grads = run_kernel(scalars, sources, weights)
    total = sum_over_tiles(grads)
    g_taps = jnp.concatenate([total[:288, :64], total[:288, 64:]])
    g_reduce = jnp.concatenate([total[288:416, :64], total[288:416, 64:]])
    g_expand = jnp.concatenate([total[416:480], total[480:544]], axis=1)
    return (out[None], grad_in[None], g_reduce[None], g_taps[None], g_expand[None])


def fine_mesh(mesh):
    shape = (mesh.devices.shape[0], mesh.devices.shape[1] // 16, 8, 2)
    return Mesh(mesh.devices.reshape(shape), ("section",) + TILE_AXES)


def solution(mesh):
    tiles = P(TILE_AXES, None, None, None)
    owned = P("section", TILE_AXES, None, None, None)
    weights = P("section", None, None)
    return jax.shard_map(
        on_device,
        mesh=fine_mesh(mesh),
        in_specs=(
            tiles, tiles, weights, weights, weights, P("section", None), P("section", None), P(), P(),
        ),
        out_specs=(owned, owned, weights, weights, weights),
        check_vma=False,
    )
```

```python
import jax
import jax.numpy as jnp
from jax import lax
from jax.experimental import pallas as pl
from jax.experimental.pallas import tpu as pltpu
from jax.sharding import Mesh
from jax.sharding import PartitionSpec as P

TILE_AXES = ("z", "y", "core")
SIDE = 16
REGION = 32
HALO = 8
RIM = 4
PIXELS = REGION * REGION
WIDTH = 64
CHANS = 256
BF = jnp.bfloat16
F32 = jnp.float32
VMEM_LIMIT = 56 * 1024 * 1024


def mm(left, right):
    return jnp.dot(left, right, preferred_element_type=F32)


def mm_first(left, right):
    return lax.dot_general(left, right, (((0,), (0,)), ((), ())), preferred_element_type=F32)


def silu_parts(value):
    sig = 0.5 + 0.5 * jnp.tanh(0.5 * value)
    out = value * sig
    return (out, sig + out * (1.0 - sig))


def around(tile, owner, near):
    north, south = (near[tile * 4], near[tile * 4 + 1])
    west, east = (near[tile * 4 + 2], near[tile * 4 + 3])

    def step(first, way, second, other):
        one = jnp.where(first >= 0, near[jnp.maximum(first, 0) * 4 + way], -1)
        two = jnp.where(second >= 0, near[jnp.maximum(second, 0) * 4 + other], -1)
        return jnp.where(one >= 0, one, two)

    ids = [
        step(north, 2, west, 0), north, step(north, 3, east, 0),
        west, tile, east,
        step(south, 2, west, 1), south, step(south, 3, east, 1),
    ]
    found = [item >= 0 for item in ids]
    rows = [owner[jnp.maximum(item, 0)] for item in ids]
    return (rows, found)


def pool_place(row, here):
    device, slot = (row >> 2, row & 3)
    gap = (device >> 1) - (here >> 1)
    side = jnp.where(gap < 0, 0, 1)
    near = jnp.where(gap == 0, 0, 4 + 4 * side) + slot
    same = (device & 1) == (here & 1)
    far = 12 + jnp.where(same, 4 * side, 0) + slot
    place = jnp.where(jnp.abs(gap) <= 1, near, far) + jnp.where(same, 0, 20)
    return jnp.clip(place, 0, 39)


def bands_of(halo):
    return (
        (HALO - halo, halo, 0, SIDE - halo),
        (HALO, SIDE, 3, 0),
        (HALO + SIDE, halo, 6, 0),
    )


def build_region(pool, region, lane, places, found, halo):
    for top, rows, first, start in bands_of(halo):
        parts = []
        for k in range(3):
            part = pool[places[first + k], pl.ds(start, rows)].astype(F32)
            part = jnp.where(found[first + k], part, 0.0)
            cut = (slice(HALO, SIDE), slice(0, SIDE), slice(0, HALO))[k]
            parts.append(part[:, cut, :])
        band = jnp.concatenate(parts, axis=1).reshape(rows * REGION, CHANS).astype(BF)
        region[pl.ds(top * REGION, rows * REGION), pl.ds(lane * CHANS, CHANS)] = band


def build_present(present, found_pair):
    for top, rows, first, _ in bands_of(HALO):
        shape = (rows * REGION, 2 * WIDTH)
        col = lax.broadcasted_iota(jnp.int32, shape, 0) % REGION
        lane = lax.broadcasted_iota(jnp.int32, shape, 1)
        sides = []
        for found in found_pair:
            flags = [jnp.where(found[first + k], 1.0, 0.0) for k in range(3)]
            sides.append(
                jnp.where(col < HALO, flags[0], jnp.where(col < HALO + SIDE, flags[1], flags[2]))
            )
        present[pl.ds(top * REGION, rows * REGION), :] = jnp.where(lane < WIDTH, sides[0], sides[1])


def build_masks(masks):
    shape = (PIXELS, 2 * WIDTH)
    pixel = lax.broadcasted_iota(jnp.int32, shape, 0)
    row, col = (pixel // REGION, pixel % REGION)
    low, high = (HALO, HALO + SIDE)
    west = (col == low) | (col == high)
    east = (col == low - 1) | (col == high - 1)
    above = (row == low - 1) | (row == high - 1)
    below = (row == low) | (row == high)
    for k, (across, along) in enumerate(
        ((above, west), (above, east), (below, west), (below, east))
    ):
        masks[k] = jnp.where(across & along, 0.0, 1.0).astype(BF)


def low_lanes(rows):
    return lax.broadcasted_iota(jnp.int32, (rows, 2 * WIDTH), 1) < WIDTH


def build_gates(gates):
    col = lax.broadcasted_iota(jnp.int32, (4 * REGION, 2 * WIDTH), 0) % REGION
    west = (col == HALO) | (col == HALO + SIDE)
    east = (col == HALO - 1) | (col == HALO + SIDE - 1)
    left = jnp.where(west & low_lanes(4 * REGION), 0.0, 1.0).astype(BF)
    gates[:, 0:128] = left
    gates[:, 128:256] = left
    gates[:, 256:384] = jnp.where(east, 0.0, 1.0).astype(BF)


def store_shifted(stack, center, start, value):
    count = value.shape[0]
    rows = pl.ds(start, count)
    low = low_lanes(count)
    other = pltpu.roll(value, WIDTH, 1)
    left = pltpu.roll(value, 1, 0)
    other_left = pltpu.roll(other, 1, 0)
    right = pltpu.roll(value, count - 1, 0)
    stack[rows, 0:128] = jnp.where(low, left, other).astype(BF)
    stack[rows, 128:256] = jnp.where(low, other_left, value).astype(BF)
    stack[rows, 256:384] = right.astype(BF)
    center[rows, :] = value.astype(BF)


def row_products(first, second, third, weights):
    one = mm(jnp.concatenate([first, third], axis=1), weights[0])
    two = mm(jnp.concatenate([second, third], axis=1), weights[1])
    low = low_lanes(first.shape[0])
    above = jnp.where(low, one[:, :128], two[:, :128])
    level = pltpu.roll(jnp.where(low, two[:, :128], one[:, :128]), WIDTH, 1)
    return (above, level, one[:, 128:] + two[:, 128:])


def convolve(stack, gates, products, start, count, weights):
    rows = pl.ds(start, count)
    parts = row_products(stack[rows, 0:128], stack[rows, 128:256], stack[rows, 256:384], weights)
    for k in range(3):
        products[k, rows, :] = parts[k]
    upper, lower = ((HALO - 1) * REGION, (HALO + SIDE - 1) * REGION)
    pair = 2 * REGION
    edge = jnp.concatenate([stack[pl.ds(upper, pair), :], stack[pl.ds(lower, pair), :]])
    edge = edge * gates[...]
    above, _, below = row_products(edge[:, 0:128], edge[:, 128:256], edge[:, 256:384], weights)
    for k, at in enumerate((upper, lower)):
        products[0, pl.ds(at, REGION), :] = above[k * pair : k * pair + REGION]
        products[2, pl.ds(at + REGION, REGION), :] = below[k * pair + REGION : (k + 1) * pair]
    inner = pl.ds(start + REGION, count - pair)
    return (
        products[0, pl.ds(start, count - pair), :]
        + products[1, inner, :]
        + products[2, pl.ds(start + pair, count - pair), :]
    )


def pool_copies(sources, pools, stored, weights, sems):
    feats, cots = ([], [])

    def add(group, source, target):
        sem = sems.at[len(feats) + len(cots)]
        group.append(pltpu.make_async_copy(source, target, sem))

    for core in range(2):
        at = 20 * core
        for source in sources[core][:3]:
            add(feats, source.at[pl.ds(0, 4)], pools[0].at[pl.ds(at, 4)])
            add(cots, source.at[pl.ds(4, 4)], pools[1].at[pl.ds(at, 4)])
            at += 4
        for source in sources[core][3:]:
            for k in range(4):
                add(feats, source.at[pl.ds(k * SIDE, SIDE)], pools[0].at[at])
                for end in range(2):
                    add(
                        cots,
                        source.at[pl.ds(4 * (SIDE + end * RIM) + k * RIM, RIM)],
                        pools[1].at[at, pl.ds(end * (SIDE - RIM), RIM)],
                    )
                at += 1
    for k, (source, target) in enumerate(zip(stored, weights)):
        add(feats if k < 3 else cots, source, target)
    return (feats, cots)


COPIES = 2 * 3 * 2 + 12 * 3 + 6


def inner_tile(region, lane):
    value = region[pl.ds(HALO * REGION, SIDE * REGION), pl.ds(lane * CHANS, CHANS)].astype(F32)
    value = value.reshape(SIDE, REGION, CHANS)[:, HALO : HALO + SIDE, :]
    return value.astype(BF)


INNER = (HALO * REGION, SIDE * REGION)


def fold_pair(value, rows, cols):
    return value[:rows, :cols] + value[rows:, cols:]


def whole_kernel(meta, owner, near, *refs):
    sources, stored, refs = ((refs[:5], refs[5:9]), refs[9:15], refs[15:])
    weights, refs = (refs[-6:], refs[:-6])
    w_red, w_tap, w_exp, v_red, v_tap, v_exp = weights
    (norms, out, grad_in, grads,
     feats, cots, sems, region, present, masks, gates, stack, center, products, s_one, s_two, s_three,
     a_own, h_one, h_two, d_one, total) = refs
    pair = pl.program_id(0)
    here, section = (meta[0], meta[1])
    copies = pool_copies(sources, (feats, cots), stored, weights, sems)

    @pl.when(pair == 0)
    def _():
        for group in copies:
            for copy in group:
                copy.start()
        build_masks(masks)
        build_gates(gates)
        total[...] = jnp.zeros_like(total)
        for copy in copies[0]:
            copy.wait()

    founds, places = ([], [])
    for lane in range(2):
        rows, found = around(meta[2 + pair * 2 + lane], owner, near)
        place = [pool_place(row, here) for row in rows]
        build_region(feats, region, lane, place, found, HALO)
        founds.append(found)
        places.append(place)
    build_present(present, founds)

    def ahead(b, carry):
        mine = b == section

        @pl.when(mine)
        def _():
            a_own[...] = region[pl.ds(*INNER), :]

        def front():
            start, count = (0, PIXELS)
            rows = pl.ds(start, count)
            pre = mm(region[rows, :], w_red[b]) * norms[b, 0:1, :128] + norms[b, 1:2, :128]
            hidden, slope = silu_parts(pre)
            there = present[rows, :]
            s_one[b, rows, :] = (slope * there * norms[b, 0:1, :128]).astype(BF)
            store_shifted(stack, center, start, hidden * there)

        front()

        def tail():
            start, count = (REGION, PIXELS - 2 * REGION)
            rows = pl.ds(start, count)
            pre = convolve(stack, gates, products, 0, PIXELS, w_tap[b])
            pre = pre * norms[b, 2:3, :128] + norms[b, 3:4, :128]
            hidden, slope = silu_parts(pre)
            s_two[b, rows, :] = (slope * norms[b, 2:3, :128]).astype(BF)
            hidden = hidden.astype(BF)

            @pl.when(mine)
            def _():
                h_two[rows, :] = hidden

            pre = (
                region[rows, :].astype(F32)
                + mm(hidden, w_exp[b]) * norms[b, 4:5, :]
                + norms[b, 5:6, :]
            )
            value, slope = silu_parts(pre)
            region[rows, :] = value.astype(BF)
            s_three[b, rows, :] = slope.astype(BF)

        tail()

        @pl.when(mine)
        def _():
            h_one[...] = center[...]
            out[0] = inner_tile(region, 0)
            out[1] = inner_tile(region, 1)

        return carry

    lax.fori_loop(0, 4, ahead, 0)

    @pl.when(pair == 0)
    def _():
        for copy in copies[1]:
            copy.wait()

    for lane in range(2):
        build_region(cots, region, lane, places[lane], founds[lane], RIM)

    def keep_inner(value):
        col = lax.broadcasted_iota(jnp.int32, value.shape, 0) % REGION
        return jnp.where((col >= HALO) & (col < HALO + SIDE), value, 0.0).astype(BF)

    def back(step, carry):
        b = 3 - step
        mine = b == section

        def first():
            start, count = (4 * REGION, PIXELS - 8 * REGION)
            rows = pl.ds(start, count)
            d_three = region[rows, :].astype(F32) * s_three[b, rows, :].astype(F32)
            e_three = (d_three * norms[b, 4:5, :]).astype(BF)
            d_two = mm(e_three, v_exp[b]) * s_two[b, rows, :].astype(F32)
            store_shifted(stack, center, start, d_two)

        first()

        @pl.when(mine)
        def _():
            rows = pl.ds(*INNER)
            d_three = region[rows, :].astype(F32) * s_three[b, rows, :].astype(F32)
            e_three = keep_inner(d_three * norms[b, 4:5, :])
            total_e = fold_pair(mm_first(h_two[rows, :], e_three), WIDTH, CHANS)
            total[416:480, :] += total_e[:, :128]
            total[480:544, :] += total_e[:, 128:]
            d_two = keep_inner(center[rows, :].astype(F32))
            around_rows = pl.ds(INNER[0] - REGION, INNER[1] + 2 * REGION)
            hidden = h_one[around_rows, :].astype(F32)
            left = pltpu.roll(hidden, 1, 0).astype(BF)
            right = pltpu.roll(hidden, hidden.shape[0] - 1, 0).astype(BF)
            middle = hidden.astype(BF)
            gated = [
                (left * masks[0, around_rows, :], 0), (middle, 0), (right * masks[1, around_rows, :], 0),
                (left, 1), (middle, 1), (right, 1),
                (left * masks[2, around_rows, :], 2), (middle, 2), (right * masks[3, around_rows, :], 2),
            ]
            for tap, (value, dy) in enumerate(gated):
                column = value[dy * REGION : dy * REGION + INNER[1]]
                piece = fold_pair(mm_first(column, d_two), WIDTH, WIDTH)
                if tap < 4:
                    total[tap * 64 : tap * 64 + 64, :64] += piece
                elif tap > 4:
                    at = (tap - 5) * 64 + 32
                    total[at : at + 64, 64:] += piece
                else:
                    total[256:288, :64] += piece[:32]
                    total[0:32, 64:] += piece[32:]

        def second():
            start, count = (5 * REGION, PIXELS - 10 * REGION)
            rows = pl.ds(start, count)
            d_hidden = convolve(
                stack, gates, products, 4 * REGION, PIXELS - 8 * REGION, v_tap[b]
            )
            d_first = (d_hidden * s_one[b, rows, :].astype(F32)).astype(BF)
            d_one[rows, :] = d_first
            d_three = region[rows, :].astype(F32) * s_three[b, rows, :].astype(F32)
            region[rows, :] = (d_three + mm(d_first, v_red[b])).astype(BF)

        second()

        @pl.when(mine)
        def _():
            rows = pl.ds(*INNER)
            d_first = keep_inner(d_one[rows, :].astype(F32))
            piece = fold_pair(mm_first(a_own[...], d_first), CHANS, WIDTH)
            total[288:416, :64] += piece[:128]
            total[288:416, 64:] += piece[128:]
            grad_in[0] = inner_tile(region, 0)
            grad_in[1] = inner_tile(region, 1)

        return carry

    lax.fori_loop(0, 4, back, 0)

    @pl.when(pair == 1)
    def _():
        grads[...] = total[...].astype(BF)


def run_kernel(scalars, sources, weights):
    def whole(item):
        return pl.BlockSpec(item.shape, lambda i, *_, n=len(item.shape): (0,) * n)

    tiles = jax.ShapeDtypeStruct((4, SIDE, SIDE, CHANS), BF)
    grads = jax.ShapeDtypeStruct((640, 128), BF)
    pair = pl.BlockSpec((2, SIDE, SIDE, CHANS), lambda i, *_: (i, 0, 0, 0))
    narrow = (PIXELS, 2 * WIDTH)
    pool = pltpu.VMEM((40, SIDE, SIDE, CHANS), BF)
    wide = (PIXELS, 2 * CHANS)
    return pl.pallas_call(
        whole_kernel,
        grid_spec=pltpu.PrefetchScalarGridSpec(
            num_scalar_prefetch=len(scalars),
            grid=(2,),
            in_specs=[pl.BlockSpec(memory_space=pl.ANY)] * (len(sources) + 6)
            + [whole(weights[6])],
            out_specs=[pair, pair, whole(grads)],
            scratch_shapes=[
                pool,
                pool,
                pltpu.SemaphoreType.DMA((COPIES,)),
                pltpu.VMEM(wide, BF),
                pltpu.VMEM(narrow, F32),
                pltpu.VMEM((4,) + narrow, BF),
                pltpu.VMEM((4 * REGION, 6 * WIDTH), BF),
                pltpu.VMEM((PIXELS, 6 * WIDTH), BF),
                pltpu.VMEM(narrow, BF),
                pltpu.VMEM((3,) + narrow, F32),
                pltpu.VMEM((4,) + narrow, BF),
                pltpu.VMEM((4,) + narrow, BF),
                pltpu.VMEM((4,) + wide, BF),
                pltpu.VMEM((INNER[1], 2 * CHANS), BF),
                pltpu.VMEM(narrow, BF),
                pltpu.VMEM(narrow, BF),
                pltpu.VMEM(narrow, BF),
                pltpu.VMEM((640, 128), F32),
                *[pltpu.VMEM(item.shape, BF) for item in weights[:6]],
            ],
        ),
        out_shape=[tiles, tiles, grads],
        compiler_params=pltpu.CompilerParams(
            dimension_semantics=("arbitrary",), vmem_limit_bytes=VMEM_LIMIT
        ),
    )(*scalars, *sources, *weights)


def shift(block, axes, distance):
    devices = range(lax.axis_size(axes))
    return lax.ppermute(block, axes, [(i, i + distance) for i in devices if i + distance in devices])


def other_core(block):
    return lax.ppermute(block, "core", [(0, 1), (1, 0)])


def trimmed(both):
    ends = (both[4:, :RIM], both[4:, SIDE - RIM :])
    return jnp.concatenate([item.reshape(-1, SIDE, CHANS) for item in (both[:4], *ends)])


def reach_close(features, cotangent):
    both = jnp.concatenate([features, cotangent])
    return [both, shift(both, TILE_AXES, 2), shift(both, TILE_AXES, -2)]


def reach_far(sent):
    return [shift(sent[0], TILE_AXES, 2), shift(sent[1], TILE_AXES, -2)]


def swap_cores(column, far, early):
    needed = jnp.where(lax.axis_index("core") == 0, far[1], far[0])
    swapped = [other_core(column[0]), early, other_core(column[2]), other_core(needed)]
    return [*column, *far, *swapped]


def swap_chunks(parts, axes):
    return lax.all_to_all(parts, axes, 0, 0, tiled=True)


def sum_over_tiles(values):
    plane = ("y", "core")
    across = lax.axis_size(plane)
    rows = values.shape[0] // across
    got = swap_chunks(values, plane).reshape(across, rows, 128)
    mine = jnp.sum(got.astype(F32), axis=0).astype(BF)
    got = swap_chunks(jnp.tile(mine, (lax.axis_size("z"), 1)), "z").reshape(-1, rows, 128)
    total = jnp.sum(got.astype(F32), axis=0).astype(BF)
    return swap_chunks(jnp.tile(total, (across, 1)), plane).astype(F32)


def split_float(value):
    high = value.astype(BF)
    low = (value - high.astype(F32)).astype(BF)
    return (high, low)


def gather_params(pieces):
    packed = jnp.concatenate([item.reshape(-1, 128) for item in pieces])
    return lax.all_gather(packed, "section", axis=0, tiled=False)


def cut_params(every, pieces):
    at = 0
    cut = []
    for item in pieces:
        rows = item.size // 128
        cut.append(every[:, at : at + rows].reshape((-1,) + item.shape[1:]))
        at += rows
    scale = cut[3].astype(F32) + cut[4].astype(F32)
    offset = cut[5].astype(F32) + cut[6].astype(F32)
    return (cut[0], cut[1], cut[2], scale, offset)


def twice(weights):
    zero = jnp.zeros_like(weights)
    return jnp.concatenate(
        [jnp.concatenate([weights, zero], axis=-1), jnp.concatenate([zero, weights], axis=-1)],
        axis=-2,
    )


def tap_pair(taps):
    blank = jnp.zeros_like(taps[:, 0, 0])

    def grid(rows, cols):
        lines = []
        for dx in rows:
            line = [blank if None in (dx, dy) else taps[:, dy, dx] for dy in cols]
            lines.append(jnp.concatenate(line, axis=2))
        return jnp.concatenate(lines, axis=1)

    return jnp.stack([grid((0, 1, 2, None), (0, 1, 2, None)), grid((0, 1, None, 2), (1, 0, None, 2))], axis=1)


def norm_rows(scale, offset):
    rows = []
    for low, high in ((0, 64), (64, 128), (128, 384)):
        for item in (scale, offset):
            part = jnp.concatenate([item[:, low:high]] * 2, axis=1)
            rows.append(jnp.pad(part, ((0, 0), (0, 512 - part.shape[1]))))
    rows.extend([jnp.zeros_like(rows[0])] * 2)
    return jnp.stack(rows, axis=1)


def on_device(
    features, out_cotangent, w_reduce, w_taps, w_expand, norm_scale, norm_shift, owner, neighbours
):
    here = lax.axis_index(TILE_AXES).astype(jnp.int32)
    section = lax.axis_index("section").astype(jnp.int32)
    slots = here * 4 + jnp.arange(4, dtype=jnp.int32)
    hit = owner[None, :] == slots[:, None]
    ids = jnp.sum(
        jnp.where(hit, jnp.arange(owner.shape[0], dtype=jnp.int32)[None, :], 0), axis=1
    )
    meta = jnp.concatenate([here[None], section[None], ids.astype(jnp.int32)])
    scalars = (meta, owner, neighbours.reshape(-1))

    pieces = [w_reduce, w_taps, w_expand, *split_float(norm_scale), *split_float(norm_shift)]
    column = reach_close(features, out_cotangent)
    every = gather_params(pieces)
    column[1], every = lax.optimization_barrier((column[1], every))
    sent = [trimmed(column[1]), trimmed(column[2])]
    column[1], sent[0] = lax.optimization_barrier((column[1], sent[0]))
    far = reach_far(sent)
    early = other_core(column[1])
    every, early = lax.optimization_barrier((every, early))
    w_red, w_tap, w_exp, scale, offset = cut_params(every, pieces)
    taps = w_tap.reshape(4, 3, 3, WIDTH, WIDTH)
    turned = taps[:, ::-1, ::-1].swapaxes(3, 4)
    weights = (
        twice(w_red),
        tap_pair(taps),
        twice(w_exp),
        twice(w_red.swapaxes(1, 2)),
        tap_pair(turned),
        twice(w_exp.swapaxes(1, 2)),
        norm_rows(scale, offset),
    )
    far, weights = lax.optimization_barrier((far, weights))
    sources = swap_cores(column, far, early)
    out, grad_in, grads = run_kernel(scalars, sources, weights)
    total = sum_over_tiles(grads)
    g_taps = jnp.concatenate([total[:288, :64], total[:288, 64:]])
    g_reduce = jnp.concatenate([total[288:416, :64], total[288:416, 64:]])
    g_expand = jnp.concatenate([total[416:480], total[480:544]], axis=1)
    return (out[None], grad_in[None], g_reduce[None], g_taps[None], g_expand[None])


def fine_mesh(mesh):
    shape = (mesh.devices.shape[0], mesh.devices.shape[1] // 16, 8, 2)
    return Mesh(mesh.devices.reshape(shape), ("section",) + TILE_AXES)


def solution(mesh):
    tiles = P(TILE_AXES, None, None, None)
    owned = P("section", TILE_AXES, None, None, None)
    weights = P("section", None, None)
    return jax.shard_map(
        on_device,
        mesh=fine_mesh(mesh),
        in_specs=(
            tiles, tiles, weights, weights, weights, P("section", None), P("section", None), P(), P(),
        ),
        out_specs=(owned, owned, weights, weights, weights),
        check_vma=False,
    )
```

```python
import jax
import jax.numpy as jnp
from jax import lax
from jax.experimental import pallas as pl
from jax.experimental.pallas import tpu as pltpu
from jax.sharding import Mesh
from jax.sharding import PartitionSpec as P

TILE_AXES = ("z", "y", "core")
SIDE = 16
REGION = 32
HALO = 8
RIM = 4
PIXELS = REGION * REGION
WIDTH = 64
CHANS = 256
BF = jnp.bfloat16
F32 = jnp.float32
VMEM_LIMIT = 56 * 1024 * 1024


def mm(left, right):
    return jnp.dot(left, right, preferred_element_type=F32)


def mm_first(left, right):
    return lax.dot_general(left, right, (((0,), (0,)), ((), ())), preferred_element_type=F32)


def silu_parts(value):
    sig = 0.5 + 0.5 * jnp.tanh(0.5 * value)
    out = value * sig
    return (out, sig + out * (1.0 - sig))


def around(tile, owner, near):
    north, south = (near[tile * 4], near[tile * 4 + 1])
    west, east = (near[tile * 4 + 2], near[tile * 4 + 3])

    def step(first, way, second, other):
        one = jnp.where(first >= 0, near[jnp.maximum(first, 0) * 4 + way], -1)
        two = jnp.where(second >= 0, near[jnp.maximum(second, 0) * 4 + other], -1)
        return jnp.where(one >= 0, one, two)

    ids = [
        step(north, 2, west, 0), north, step(north, 3, east, 0),
        west, tile, east,
        step(south, 2, west, 1), south, step(south, 3, east, 1),
    ]
    found = [item >= 0 for item in ids]
    rows = [owner[jnp.maximum(item, 0)] for item in ids]
    return (rows, found)


def pool_place(row, here):
    device, slot = (row >> 2, row & 3)
    gap = (device >> 1) - (here >> 1)
    side = jnp.where(gap < 0, 0, 1)
    near = jnp.where(gap == 0, 0, 4 + 4 * side) + slot
    place = jnp.where(jnp.abs(gap) <= 1, near, 12 + 4 * side + slot)
    place = place + jnp.where((device & 1) == (here & 1), 0, 20)
    return jnp.clip(place, 0, 39)


def bands_of(halo):
    return (
        (HALO - halo, halo, 0, SIDE - halo),
        (HALO, SIDE, 3, 0),
        (HALO + SIDE, halo, 6, 0),
    )


def build_region(pool, region, lane, places, found, halo):
    for top, rows, first, start in bands_of(halo):
        parts = []
        for k in range(3):
            part = pool[places[first + k], pl.ds(start, rows)].astype(F32)
            part = jnp.where(found[first + k], part, 0.0)
            cut = (slice(HALO, SIDE), slice(0, SIDE), slice(0, HALO))[k]
            parts.append(part[:, cut, :])
        band = jnp.concatenate(parts, axis=1).reshape(rows * REGION, CHANS).astype(BF)
        region[pl.ds(top * REGION, rows * REGION), pl.ds(lane * CHANS, CHANS)] = band


def build_present(present, found_pair):
    for top, rows, first, _ in bands_of(HALO):
        shape = (rows * REGION, 2 * WIDTH)
        col = lax.broadcasted_iota(jnp.int32, shape, 0) % REGION
        lane = lax.broadcasted_iota(jnp.int32, shape, 1)
        sides = []
        for found in found_pair:
            flags = [jnp.where(found[first + k], 1.0, 0.0) for k in range(3)]
            sides.append(
                jnp.where(col < HALO, flags[0], jnp.where(col < HALO + SIDE, flags[1], flags[2]))
            )
        present[pl.ds(top * REGION, rows * REGION), :] = jnp.where(lane < WIDTH, sides[0], sides[1])


def build_masks(masks):
    shape = (PIXELS, 2 * WIDTH)
    pixel = lax.broadcasted_iota(jnp.int32, shape, 0)
    row, col = (pixel // REGION, pixel % REGION)
    low, high = (HALO, HALO + SIDE)
    west = (col == low) | (col == high)
    east = (col == low - 1) | (col == high - 1)
    above = (row == low - 1) | (row == high - 1)
    below = (row == low) | (row == high)
    for k, (across, along) in enumerate(
        ((above, west), (above, east), (below, west), (below, east))
    ):
        masks[k] = jnp.where(across & along, 0.0, 1.0).astype(BF)


def low_lanes(rows):
    return lax.broadcasted_iota(jnp.int32, (rows, 2 * WIDTH), 1) < WIDTH


def build_gates(gates):
    col = lax.broadcasted_iota(jnp.int32, (4 * REGION, 2 * WIDTH), 0) % REGION
    west = (col == HALO) | (col == HALO + SIDE)
    east = (col == HALO - 1) | (col == HALO + SIDE - 1)
    left = jnp.where(west & low_lanes(4 * REGION), 0.0, 1.0).astype(BF)
    gates[:, 0:128] = left
    gates[:, 128:256] = left
    gates[:, 256:384] = jnp.where(east, 0.0, 1.0).astype(BF)


def store_shifted(stack, center, start, value):
    count = value.shape[0]
    rows = pl.ds(start, count)
    low = low_lanes(count)
    other = pltpu.roll(value, WIDTH, 1)
    left = pltpu.roll(value, 1, 0)
    other_left = pltpu.roll(other, 1, 0)
    right = pltpu.roll(value, count - 1, 0)
    stack[rows, 0:128] = jnp.where(low, left, other).astype(BF)
    stack[rows, 128:256] = jnp.where(low, other_left, value).astype(BF)
    stack[rows, 256:384] = right.astype(BF)
    center[rows, :] = value.astype(BF)


def row_products(first, second, third, weights):
    one = mm(jnp.concatenate([first, third], axis=1), weights[0])
    two = mm(jnp.concatenate([second, third], axis=1), weights[1])
    low = low_lanes(first.shape[0])
    above = jnp.where(low, one[:, :128], two[:, :128])
    level = pltpu.roll(jnp.where(low, two[:, :128], one[:, :128]), WIDTH, 1)
    return (above, level, one[:, 128:] + two[:, 128:])


def convolve(stack, gates, products, start, count, weights):
    rows = pl.ds(start, count)
    parts = row_products(stack[rows, 0:128], stack[rows, 128:256], stack[rows, 256:384], weights)
    for k in range(3):
        products[k, rows, :] = parts[k]
    upper, lower = ((HALO - 1) * REGION, (HALO + SIDE - 1) * REGION)
    pair = 2 * REGION
    edge = jnp.concatenate([stack[pl.ds(upper, pair), :], stack[pl.ds(lower, pair), :]])
    edge = edge * gates[...]
    above, _, below = row_products(edge[:, 0:128], edge[:, 128:256], edge[:, 256:384], weights)
    for k, at in enumerate((upper, lower)):
        products[0, pl.ds(at, REGION), :] = above[k * pair : k * pair + REGION]
        products[2, pl.ds(at + REGION, REGION), :] = below[k * pair + REGION : (k + 1) * pair]
    inner = pl.ds(start + REGION, count - pair)
    return (
        products[0, pl.ds(start, count - pair), :]
        + products[1, inner, :]
        + products[2, pl.ds(start + pair, count - pair), :]
    )


def pool_copies(sources, pools, stored, weights, sems):
    feats, cots = ([], [])

    def add(group, source, target):
        sem = sems.at[len(feats) + len(cots)]
        group.append(pltpu.make_async_copy(source, target, sem))

    for core in range(2):
        at = 20 * core
        for source in sources[core][:3]:
            add(feats, source.at[pl.ds(0, 4)], pools[0].at[pl.ds(at, 4)])
            add(cots, source.at[pl.ds(4, 4)], pools[1].at[pl.ds(at, 4)])
            at += 4
        for source in sources[core][3:]:
            for k in range(4):
                add(feats, source.at[pl.ds(k * SIDE, SIDE)], pools[0].at[at])
                for end in range(2):
                    add(
                        cots,
                        source.at[pl.ds(4 * (SIDE + end * RIM) + k * RIM, RIM)],
                        pools[1].at[at, pl.ds(end * (SIDE - RIM), RIM)],
                    )
                at += 1
    for k, (source, target) in enumerate(zip(stored, weights)):
        add(feats if k < 3 else cots, source, target)
    return (feats, cots)


COPIES = 2 * (3 * 2 + 8 * 3) + 6


def inner_tile(region, lane):
    value = region[pl.ds(HALO * REGION, SIDE * REGION), pl.ds(lane * CHANS, CHANS)].astype(F32)
    value = value.reshape(SIDE, REGION, CHANS)[:, HALO : HALO + SIDE, :]
    return value.astype(BF)


INNER = (HALO * REGION, SIDE * REGION)


def fold_pair(value, rows, cols):
    return value[:rows, :cols] + value[rows:, cols:]


def whole_kernel(meta, owner, near, *refs):
    sources, stored, refs = ((refs[:5], refs[5:10]), refs[10:16], refs[16:])
    weights, refs = (refs[-6:], refs[:-6])
    w_red, w_tap, w_exp, v_red, v_tap, v_exp = weights
    (norms, out, grad_in, grads,
     feats, cots, sems, region, present, masks, gates, stack, center, products, s_one, s_two, s_three,
     a_own, h_one, h_two, d_one, total) = refs
    pair = pl.program_id(0)
    here, section = (meta[0], meta[1])
    copies = pool_copies(sources, (feats, cots), stored, weights, sems)

    @pl.when(pair == 0)
    def _():
        for group in copies:
            for copy in group:
                copy.start()
        build_masks(masks)
        build_gates(gates)
        total[...] = jnp.zeros_like(total)
        for copy in copies[0]:
            copy.wait()

    founds, places = ([], [])
    for lane in range(2):
        rows, found = around(meta[2 + pair * 2 + lane], owner, near)
        place = [pool_place(row, here) for row in rows]
        build_region(feats, region, lane, place, found, HALO)
        founds.append(found)
        places.append(place)
    build_present(present, founds)

    def ahead(b, carry):
        mine = b == section

        @pl.when(mine)
        def _():
            a_own[...] = region[pl.ds(*INNER), :]

        def front():
            start, count = (0, PIXELS)
            rows = pl.ds(start, count)
            pre = mm(region[rows, :], w_red[b]) * norms[b, 0:1, :128] + norms[b, 1:2, :128]
            hidden, slope = silu_parts(pre)
            there = present[rows, :]
            s_one[b, rows, :] = (slope * there * norms[b, 0:1, :128]).astype(BF)
            store_shifted(stack, center, start, hidden * there)

        front()

        def tail():
            start, count = (REGION, PIXELS - 2 * REGION)
            rows = pl.ds(start, count)
            pre = convolve(stack, gates, products, 0, PIXELS, w_tap[b])
            pre = pre * norms[b, 2:3, :128] + norms[b, 3:4, :128]
            hidden, slope = silu_parts(pre)
            s_two[b, rows, :] = (slope * norms[b, 2:3, :128]).astype(BF)
            hidden = hidden.astype(BF)

            @pl.when(mine)
            def _():
                h_two[rows, :] = hidden

            pre = (
                region[rows, :].astype(F32)
                + mm(hidden, w_exp[b]) * norms[b, 4:5, :]
                + norms[b, 5:6, :]
            )
            value, slope = silu_parts(pre)
            region[rows, :] = value.astype(BF)
            s_three[b, rows, :] = slope.astype(BF)

        tail()

        @pl.when(mine)
        def _():
            h_one[...] = center[...]
            out[0] = inner_tile(region, 0)
            out[1] = inner_tile(region, 1)

        return carry

    lax.fori_loop(0, 4, ahead, 0)

    @pl.when(pair == 0)
    def _():
        for copy in copies[1]:
            copy.wait()

    for lane in range(2):
        build_region(cots, region, lane, places[lane], founds[lane], RIM)

    def keep_inner(value):
        col = lax.broadcasted_iota(jnp.int32, value.shape, 0) % REGION
        return jnp.where((col >= HALO) & (col < HALO + SIDE), value, 0.0).astype(BF)

    def back(step, carry):
        b = 3 - step
        mine = b == section

        def first():
            start, count = (4 * REGION, PIXELS - 8 * REGION)
            rows = pl.ds(start, count)
            d_three = region[rows, :].astype(F32) * s_three[b, rows, :].astype(F32)
            e_three = (d_three * norms[b, 4:5, :]).astype(BF)
            d_two = mm(e_three, v_exp[b]) * s_two[b, rows, :].astype(F32)
            store_shifted(stack, center, start, d_two)

        first()

        @pl.when(mine)
        def _():
            rows = pl.ds(*INNER)
            d_three = region[rows, :].astype(F32) * s_three[b, rows, :].astype(F32)
            e_three = keep_inner(d_three * norms[b, 4:5, :])
            total_e = fold_pair(mm_first(h_two[rows, :], e_three), WIDTH, CHANS)
            total[416:480, :] += total_e[:, :128]
            total[480:544, :] += total_e[:, 128:]
            d_two = keep_inner(center[rows, :].astype(F32))
            around_rows = pl.ds(INNER[0] - REGION, INNER[1] + 2 * REGION)
            hidden = h_one[around_rows, :].astype(F32)
            left = pltpu.roll(hidden, 1, 0).astype(BF)
            right = pltpu.roll(hidden, hidden.shape[0] - 1, 0).astype(BF)
            middle = hidden.astype(BF)
            gated = [
                (left * masks[0, around_rows, :], 0), (middle, 0), (right * masks[1, around_rows, :], 0),
                (left, 1), (middle, 1), (right, 1),
                (left * masks[2, around_rows, :], 2), (middle, 2), (right * masks[3, around_rows, :], 2),
            ]
            for tap, (value, dy) in enumerate(gated):
                column = value[dy * REGION : dy * REGION + INNER[1]]
                piece = fold_pair(mm_first(column, d_two), WIDTH, WIDTH)
                if tap < 4:
                    total[tap * 64 : tap * 64 + 64, :64] += piece
                elif tap > 4:
                    at = (tap - 5) * 64 + 32
                    total[at : at + 64, 64:] += piece
                else:
                    total[256:288, :64] += piece[:32]
                    total[0:32, 64:] += piece[32:]

        def second():
            start, count = (5 * REGION, PIXELS - 10 * REGION)
            rows = pl.ds(start, count)
            d_hidden = convolve(
                stack, gates, products, 4 * REGION, PIXELS - 8 * REGION, v_tap[b]
            )
            d_first = (d_hidden * s_one[b, rows, :].astype(F32)).astype(BF)
            d_one[rows, :] = d_first
            d_three = region[rows, :].astype(F32) * s_three[b, rows, :].astype(F32)
            region[rows, :] = (d_three + mm(d_first, v_red[b])).astype(BF)

        second()

        @pl.when(mine)
        def _():
            rows = pl.ds(*INNER)
            d_first = keep_inner(d_one[rows, :].astype(F32))
            piece = fold_pair(mm_first(a_own[...], d_first), CHANS, WIDTH)
            total[288:416, :64] += piece[:128]
            total[288:416, 64:] += piece[128:]
            grad_in[0] = inner_tile(region, 0)
            grad_in[1] = inner_tile(region, 1)

        return carry

    lax.fori_loop(0, 4, back, 0)

    @pl.when(pair == 1)
    def _():
        grads[...] = total[...].astype(BF)


def run_kernel(scalars, sources, weights):
    def whole(item):
        return pl.BlockSpec(item.shape, lambda i, *_, n=len(item.shape): (0,) * n)

    tiles = jax.ShapeDtypeStruct((4, SIDE, SIDE, CHANS), BF)
    grads = jax.ShapeDtypeStruct((640, 128), BF)
    pair = pl.BlockSpec((2, SIDE, SIDE, CHANS), lambda i, *_: (i, 0, 0, 0))
    narrow = (PIXELS, 2 * WIDTH)
    pool = pltpu.VMEM((40, SIDE, SIDE, CHANS), BF)
    wide = (PIXELS, 2 * CHANS)
    return pl.pallas_call(
        whole_kernel,
        grid_spec=pltpu.PrefetchScalarGridSpec(
            num_scalar_prefetch=len(scalars),
            grid=(2,),
            in_specs=[pl.BlockSpec(memory_space=pl.ANY)] * (len(sources) + 6)
            + [whole(weights[6])],
            out_specs=[pair, pair, whole(grads)],
            scratch_shapes=[
                pool,
                pool,
                pltpu.SemaphoreType.DMA((COPIES,)),
                pltpu.VMEM(wide, BF),
                pltpu.VMEM(narrow, F32),
                pltpu.VMEM((4,) + narrow, BF),
                pltpu.VMEM((4 * REGION, 6 * WIDTH), BF),
                pltpu.VMEM((PIXELS, 6 * WIDTH), BF),
                pltpu.VMEM(narrow, BF),
                pltpu.VMEM((3,) + narrow, F32),
                pltpu.VMEM((4,) + narrow, BF),
                pltpu.VMEM((4,) + narrow, BF),
                pltpu.VMEM((4,) + wide, BF),
                pltpu.VMEM((INNER[1], 2 * CHANS), BF),
                pltpu.VMEM(narrow, BF),
                pltpu.VMEM(narrow, BF),
                pltpu.VMEM(narrow, BF),
                pltpu.VMEM((640, 128), F32),
                *[pltpu.VMEM(item.shape, BF) for item in weights[:6]],
            ],
        ),
        out_shape=[tiles, tiles, grads],
        compiler_params=pltpu.CompilerParams(
            dimension_semantics=("arbitrary",), vmem_limit_bytes=VMEM_LIMIT
        ),
    )(*scalars, *sources, *weights)


def shift(block, axes, distance):
    devices = range(lax.axis_size(axes))
    return lax.ppermute(block, axes, [(i, i + distance) for i in devices if i + distance in devices])


def other_core(block):
    return lax.ppermute(block, "core", [(0, 1), (1, 0)])


def trimmed(both):
    ends = (both[4:, :RIM], both[4:, SIDE - RIM :])
    return jnp.concatenate([item.reshape(-1, SIDE, CHANS) for item in (both[:4], *ends)])


def exchange(features, cotangent):
    both = jnp.concatenate([features, cotangent])
    column = [both]
    for distance in (2, -2):
        column.append(shift(both, TILE_AXES, distance))
    for k, distance in ((1, 2), (2, -2)):
        column.append(shift(trimmed(column[k]), TILE_AXES, distance))
    return column + [other_core(item) for item in column]


def swap_chunks(parts, axes):
    return lax.all_to_all(parts, axes, 0, 0, tiled=True)


def sum_over_tiles(values):
    plane = ("y", "core")
    across = lax.axis_size(plane)
    rows = values.shape[0] // across
    got = swap_chunks(values, plane).reshape(across, rows, 128)
    mine = jnp.sum(got.astype(F32), axis=0).astype(BF)
    got = swap_chunks(jnp.tile(mine, (lax.axis_size("z"), 1)), "z").reshape(-1, rows, 128)
    total = jnp.sum(got.astype(F32), axis=0).astype(BF)
    return swap_chunks(jnp.tile(total, (across, 1)), plane).astype(F32)


def split_float(value):
    high = value.astype(BF)
    low = (value - high.astype(F32)).astype(BF)
    return (high, low)


def gather_params(w_reduce, w_taps, w_expand, norm_scale, norm_shift):
    pieces = [w_reduce, w_taps, w_expand]
    for item in (norm_scale, norm_shift):
        pieces.extend(split_float(item))
    packed = jnp.concatenate([item.reshape(-1, 128) for item in pieces])
    every = lax.all_gather(packed, "section", axis=0, tiled=False)
    at = 0
    cut = []
    for item in pieces:
        rows = item.size // 128
        cut.append(every[:, at : at + rows].reshape((-1,) + item.shape[1:]))
        at += rows
    scale = cut[3].astype(F32) + cut[4].astype(F32)
    offset = cut[5].astype(F32) + cut[6].astype(F32)
    return (cut[0], cut[1], cut[2], scale, offset)


def twice(weights):
    zero = jnp.zeros_like(weights)
    return jnp.concatenate(
        [jnp.concatenate([weights, zero], axis=-1), jnp.concatenate([zero, weights], axis=-1)],
        axis=-2,
    )


def tap_pair(taps):
    blank = jnp.zeros_like(taps[:, 0, 0])

    def grid(rows, cols):
        lines = []
        for dx in rows:
            line = [blank if None in (dx, dy) else taps[:, dy, dx] for dy in cols]
            lines.append(jnp.concatenate(line, axis=2))
        return jnp.concatenate(lines, axis=1)

    return jnp.stack([grid((0, 1, 2, None), (0, 1, 2, None)), grid((0, 1, None, 2), (1, 0, None, 2))], axis=1)


def norm_rows(scale, offset):
    rows = []
    for low, high in ((0, 64), (64, 128), (128, 384)):
        for item in (scale, offset):
            part = jnp.concatenate([item[:, low:high]] * 2, axis=1)
            rows.append(jnp.pad(part, ((0, 0), (0, 512 - part.shape[1]))))
    rows.extend([jnp.zeros_like(rows[0])] * 2)
    return jnp.stack(rows, axis=1)


def on_device(
    features, out_cotangent, w_reduce, w_taps, w_expand, norm_scale, norm_shift, owner, neighbours
):
    here = lax.axis_index(TILE_AXES).astype(jnp.int32)
    section = lax.axis_index("section").astype(jnp.int32)
    slots = here * 4 + jnp.arange(4, dtype=jnp.int32)
    hit = owner[None, :] == slots[:, None]
    ids = jnp.sum(
        jnp.where(hit, jnp.arange(owner.shape[0], dtype=jnp.int32)[None, :], 0), axis=1
    )
    meta = jnp.concatenate([here[None], section[None], ids.astype(jnp.int32)])
    scalars = (meta, owner, neighbours.reshape(-1))

    sources = exchange(features, out_cotangent)
    w_red, w_tap, w_exp, scale, offset = gather_params(
        w_reduce, w_taps, w_expand, norm_scale, norm_shift
    )
    taps = w_tap.reshape(4, 3, 3, WIDTH, WIDTH)
    turned = taps[:, ::-1, ::-1].swapaxes(3, 4)
    weights = (
        twice(w_red),
        tap_pair(taps),
        twice(w_exp),
        twice(w_red.swapaxes(1, 2)),
        tap_pair(turned),
        twice(w_exp.swapaxes(1, 2)),
        norm_rows(scale, offset),
    )
    out, grad_in, grads = run_kernel(scalars, sources, weights)
    total = sum_over_tiles(grads)
    g_taps = jnp.concatenate([total[:288, :64], total[:288, 64:]])
    g_reduce = jnp.concatenate([total[288:416, :64], total[288:416, 64:]])
    g_expand = jnp.concatenate([total[416:480], total[480:544]], axis=1)
    return (out[None], grad_in[None], g_reduce[None], g_taps[None], g_expand[None])


def fine_mesh(mesh):
    shape = (mesh.devices.shape[0], mesh.devices.shape[1] // 16, 8, 2)
    return Mesh(mesh.devices.reshape(shape), ("section",) + TILE_AXES)


def solution(mesh):
    tiles = P(TILE_AXES, None, None, None)
    owned = P("section", TILE_AXES, None, None, None)
    weights = P("section", None, None)
    return jax.shard_map(
        on_device,
        mesh=fine_mesh(mesh),
        in_specs=(
            tiles, tiles, weights, weights, weights, P("section", None), P("section", None), P(), P(),
        ),
        out_specs=(owned, owned, weights, weights, weights),
        check_vma=False,
    )
```
